256 devices in a mesh: rows: 32 (over y, z), rhs: 8 (over x, core).
Axes of the slice: x: 4, y: 4, z: 8, core: 2. Of those that a mesh axis runs over, the one named last changes fastest.
Arguments:
- lower_panels: bfloat16 [131072, 1024], P('rows', 'rhs'), may hold values from -0.03125 to 0.03125
- parent_solution: bfloat16 [131072, 2048], P('rows', 'rhs'), may hold values from -6 to 6
- parent_rows: int32 [131072], P('rows'), may hold values from 0 to 131071, as said below
- live_counts: int32 [32], P('rows'), may hold values from 512 to 4096, as said below
- front_rhs: bfloat16 [1024, 2048], P('rows', 'rhs'), may hold values from -6 to 6
- coupling: float32 [512, 512], replicated, may hold values from -0.25 to 0.25
- inverse_one: float32 [512, 512], replicated, as said below
- inverse_two: float32 [512, 512], replicated, as said below
Outputs:
- solution: float32 [1024, 2048], P('rows', 'rhs')
The draws below stay inside these ranges and needn't reach their ends.
Inputs may be any that keep to these rules, and one draw needn't show every extreme that they name: `parent_rows`: the 128 entries of an aligned block of one device's 4096 entries all lie among the 4096 rows of one index of rows, the block's owner; two blocks of one device have the same owner exactly when their block numbers differ by a multiple of 32. `live_counts`: the live rows of an index are its first ones. Each count is 4096 divided by 1, 2, 4 or 8, and some index has all 4096. `inverse_one`: upper triangular. `inverse_two`: upper triangular.
All inputs are finite; a program needn't handle non-finite values.
Results may differ from the reference program's by a relative error of at most 0.0003.
Values may be sent and summed in bfloat16 or wider, within the bound.
A program may use at most 64 MiB of HBM per device.

```python
import math
import jax
import jax.numpy as jnp
from jax import lax

PANEL = 512
R = 2048
BLK = 128
ROWS_DEV = 4096
ROWS = 131072
N_ROWS = 32


def draw_parent_rows(key, part):
    block_count = ROWS_DEV // BLK
    device_keys = jax.random.split(jax.random.fold_in(key, 11), N_ROWS)
    orders = jax.vmap(lambda one_key: jax.random.permutation(one_key, N_ROWS))(device_keys)
    owners = orders[:, jnp.arange(block_count) % N_ROWS]
    offsets = jax.random.randint(jax.random.fold_in(key, 12), (N_ROWS, block_count, BLK), 0, ROWS_DEV)
    chosen = owners[:, :, None] * ROWS_DEV + offsets
    return chosen.reshape(ROWS).astype(jnp.int32)


def draw_live_counts(key, part):
    shifts = jax.random.randint(jax.random.fold_in(key, 21), (N_ROWS,), 0, 4)
    fullest = jax.random.randint(jax.random.fold_in(key, 22), (), 0, N_ROWS)
    shifts = jnp.where(jnp.arange(N_ROWS) == fullest, 0, shifts)
    return jnp.right_shift(jnp.full((N_ROWS,), ROWS_DEV, jnp.int32), shifts.astype(jnp.int32)).astype(jnp.int32)


def triangle(key):
    diag_key, off_key = jax.random.split(key, 2)
    diagonal = jax.random.uniform(diag_key, (PANEL,), jnp.float32, 0.5, 1.5)
    offdiag = jax.random.normal(off_key, (PANEL, PANEL), jnp.float32) * (0.6 / math.sqrt(PANEL))
    matrix = jnp.triu(offdiag, 1) + jnp.diag(diagonal)
    return matrix


def draw_inverse_one(key, part):
    return triangle(jax.random.fold_in(key, 31))


def draw_inverse_two(key, part):
    return triangle(jax.random.fold_in(key, 32))


def spiked(array, stream_key, source, target, parts, factor):
    def block_of(dim):
        return (jnp.arange(array.shape[dim]) // (array.shape[dim] // parts)).reshape((-1,) + (1,) * (array.ndim - 1 - dim))

    one_side = jax.random.permutation(stream_key, parts)[block_of(target)]
    other_side = (block_of(target) + parts // 2) % parts
    return jnp.where((block_of(source) == one_side) | (block_of(source) == other_side), factor * array, array)


def shard_levels(rng, shape, cuts, smallest, high):
    loudness = 1.0
    for axis_at, blocks in cuts:
        steps = jax.random.uniform(jax.random.fold_in(jax.random.fold_in(rng, 6), axis_at), (blocks,), jnp.float32, smallest / len(cuts), high / len(cuts))
        loudness = loudness * jnp.repeat(jnp.exp(steps), shape[axis_at] // blocks).reshape((-1,) + (1,) * (len(shape) - 1 - axis_at))
    return loudness


def normal_values(own_key, dims, spread, limit, shards=(), kind=jnp.bfloat16):
    result = jax.random.normal(own_key, dims, jnp.float32) * spread
    if len(shards) > 0:
        result = shard_levels(own_key, dims, shards, -0.22, 0.18) * result
    return jnp.clip(result, min=-limit, max=limit).astype(kind)


def heavy_noise(key, dims, spread, most, shards, heavy, held_as=jnp.bfloat16):
    values = spread * jax.random.normal(key, dims, jnp.float32)
    if shards:
        values = values * shard_levels(key, dims, shards, -0.22, 0.18)
    return jnp.clip(spiked(values, jax.random.fold_in(key, 3), *heavy), -most, most).astype(held_as)


def setup_inputs(seed: int = 0) -> dict:
    splits = jax.random.split(jax.random.key(seed), 9)
    return {
        "lower_panels": heavy_noise(splits[0], (ROWS, 2 * PANEL), ROWS ** -0.5, 0.03125, ((0, 32), (1, 8)), (0, 1, 32, 2.75)),
        "parent_solution": normal_values(splits[1], (ROWS, R), 1.0, 6.0, ((0, 32), (1, 8))),
        "parent_rows": draw_parent_rows(jax.random.fold_in(splits[8], 71), 0),
        "live_counts": draw_live_counts(jax.random.fold_in(splits[8], 71), 0),
        "front_rhs": normal_values(splits[4], (2 * PANEL, R), 1.0, 6.0, ((0, 32), (1, 8))),
        "coupling": normal_values(splits[5], (PANEL, PANEL), PANEL ** -0.5, 0.25, (), jnp.float32),
        "inverse_one": draw_inverse_one(jax.random.fold_in(splits[8], 71), 0),
        "inverse_two": draw_inverse_two(jax.random.fold_in(splits[8], 71), 0),
    }


def reference(lower_panels, parent_solution, parent_rows, live_counts, front_rhs, coupling, inverse_one, inverse_two):
    row_lists = parent_rows.reshape(N_ROWS, ROWS_DEV)
    positions = jnp.arange(ROWS_DEV, dtype=jnp.int32)

    def add_block(total, inputs):
        device, chosen, count = inputs
        fetched = parent_solution[chosen]
        fetched = jnp.where((positions < count)[:, None], fetched, jnp.zeros((), fetched.dtype))
        panel = lax.dynamic_slice_in_dim(lower_panels, (device * ROWS_DEV).astype(jnp.int32), ROWS_DEV, 0)
        term = jnp.dot(panel.T.astype(jnp.float32), fetched.astype(jnp.float32), precision=lax.Precision.HIGHEST)
        return total + term, None

    start_total = jnp.zeros((2 * PANEL, R), jnp.float32)
    total, _ = lax.scan(add_block, start_total, (jnp.arange(N_ROWS, dtype=jnp.int32), row_lists, live_counts))
    residual = front_rhs.astype(jnp.float32) - total
    second = jnp.dot(inverse_two, residual[PANEL:], precision=lax.Precision.HIGHEST)
    reduced = residual[:PANEL] - jnp.dot(coupling, second, precision=lax.Precision.HIGHEST)
    first = jnp.dot(inverse_one, reduced, precision=lax.Precision.HIGHEST)
    return jnp.concatenate([first, second], axis=0)
```

```python
import functools

import jax
import jax.numpy as jnp
from jax import lax
from jax.experimental import pallas as pl
from jax.experimental.pallas import tpu as pltpu
from jax.sharding import PartitionSpec as P

BLK = 128
TILE = 128
PLANE = (4, 8)
RING = 4
GROUP = 4
MESH = pl.DeviceIdType.MESH


def offsets(plane):
    size_y, size_z = plane
    pairs = [(dy, dz) for dy in range(size_y) for dz in range(size_z)]
    return sorted(
        pairs, key=lambda p: (min(p[0], size_y - p[0]) + min(p[1], size_z - p[1]), p)
    )


def kernel(
    plane,
    blocks_ref,
    rows_ref,
    parent_ref,
    rhs_ref,
    coupling_hbm,
    inverse_one_hbm,
    inverse_two_hbm,
    out_ref,
    panels,
    row_buf,
    row_smem,
    staged,
    wide,
    picked,
    fetched,
    product,
    shares,
    coupling,
    inverse_one,
    inverse_two,
    solved,
    returned,
    turned,
    load_sem,
    smem_sem,
    self_sem,
    row_send,
    row_recv,
    blk_send,
    blk_recv,
    near_send,
    near_recv,
    far_send,
    far_recv,
    twin_send,
    twin_recv,
    sum_send,
    sum_recv,
    out_send,
    out_recv,
):
    size_y, size_z = plane
    count = size_y * size_z
    groups = count // GROUP
    offs = offsets(plane)
    me = lax.axis_index("rows")
    side = lax.axis_index("rhs")
    y, z = me // size_z, me % size_z
    x, core = side // 2, side % 2
    right = ((x + 1) % RING) * 2 + core
    left = ((x + RING - 1) % RING) * 2 + core
    opposite = ((x + 2) % RING) * 2 + core
    twin = x * 2 + (1 - core)

    def target(t):
        dy, dz = offs[t]
        return ((y + size_y - dy) % size_y) * size_z + (z + size_z - dz) % size_z

    def source(t):
        dy, dz = offs[t]
        return ((y + dy) % size_y) * size_z + (z + dz) % size_z

    def remote(src, dst, send, recv, **device):
        return pltpu.make_async_remote_copy(
            src_ref=src, dst_ref=dst, send_sem=send, recv_sem=recv,
            device_id=device, device_id_type=MESH,
        )

    barrier = pltpu.get_barrier_semaphore()
    for t in range(1, count):
        pl.semaphore_signal(barrier, inc=1, device_id={"rows": target(t)}, device_id_type=MESH)
    for other in (left, right, twin):
        pl.semaphore_signal(barrier, inc=1, device_id={"rhs": other}, device_id_type=MESH)

    loads = [
        pltpu.make_async_copy(parent_ref, staged, load_sem.at[0]),
        pltpu.make_async_copy(coupling_hbm, coupling, load_sem.at[1]),
        pltpu.make_async_copy(inverse_one_hbm, inverse_one, load_sem.at[2]),
        pltpu.make_async_copy(inverse_two_hbm, inverse_two, load_sem.at[3]),
    ]
    for load in loads:
        load.start()
    own_block = pltpu.make_async_copy(blocks_ref.at[me], panels.at[side, 0], self_sem.at[0])
    own_block.start()
    own_rows = pltpu.make_async_copy(rows_ref.at[me], row_buf.at[0], self_sem.at[1])
    own_rows.start()

    pl.semaphore_wait(barrier, count + 2)

    row_copies, blk_copies = [], []
    for t in range(1, count):
        copy = remote(rows_ref.at[target(t)], row_buf.at[t], row_send.at[t], row_recv.at[t], rows=target(t))
        copy.start()
        row_copies.append(copy)
    for t in range(1, count):
        copy = remote(
            blocks_ref.at[target(t)], panels.at[side, t], blk_send.at[t], blk_recv.at[t], rows=target(t)
        )
        copy.start()
        blk_copies.append(copy)

    def part(cls, g):
        return panels.at[cls, pl.ds(g * GROUP, GROUP)]

    def near(direction, cls, g):
        other = right if direction == 0 else left
        return remote(part(cls, g), part(cls, g), near_send.at[direction, g], near_recv.at[direction, g], rhs=other)

    def far(cls, g):
        other = right if g % 2 == 0 else left
        return remote(part(cls, g), part(cls, g), far_send.at[g], far_recv.at[g], rhs=other)

    def pair(slot, cls, g):
        return remote(part(cls, g), part(cls, g), twin_send.at[slot, g], twin_recv.at[slot, g], rhs=twin)

    loads[0].wait()
    depth = wide.shape[0]
    step = 256

    def widen(i, carry):
        at = pl.ds(pl.multiple_of(i * step, step), step)
        wide[at, :] = staged[at, :].astype(jnp.float32)
        return carry

    lax.fori_loop(0, depth // step, widen, 0)

    own_rows.wait()
    for copy in row_copies:
        copy.wait_recv()
    to_smem = pltpu.make_async_copy(row_buf, row_smem, smem_sem)
    to_smem.start()
    to_smem.wait()

    def gather(t):
        def eight(i, carry):
            for u in range(8):
                at = row_smem[t, 0, i * 8 + u]
                picked[pl.ds(i * 8 + u, 1), :] = wide[pl.ds(at, 1), :]
            return carry

        lax.fori_loop(0, BLK // 8, eight, 0)
        fetched[t] = picked[...].T.astype(jnp.bfloat16)

    def gather_group(g):
        def one(k, carry):
            gather(g * GROUP + k)
            return carry

        lax.fori_loop(0, GROUP, one, 0)

    for g in range(groups + 2):
        if g < groups:
            for t in range(g * GROUP, (g + 1) * GROUP):
                if t == 0:
                    own_block.wait()
                else:
                    blk_copies[t - 1].wait_recv()
            near(0, side, g).start()
            near(1, side, g).start()
            pair(0, side, g).start()
        if 1 <= g <= groups:
            near(0, left, g - 1).wait_recv()
            if (g - 1) % 2 == 0:
                far(left, g - 1).start()
            pair(1, left, g - 1).start()
            near(1, right, g - 1).wait_recv()
            if (g - 1) % 2 == 1:
                far(right, g - 1).start()
            pair(2, right, g - 1).start()
        if g >= 2:
            far(opposite, g - 2).wait_recv()
            pair(3, opposite, g - 2).start()
        if g < groups:
            gather_group(g)

    acc_cols = product.shape[0]
    chips = [x, (x + RING - 1) % RING, (x + 1) % RING, (x + 2) % RING]
    for slot, chip in enumerate(chips):
        for g in range(groups):
            pair(slot, chip * 2 + (1 - core), g).wait_recv()

        def accumulate(g, total, chip=chip):
            at = pl.ds(g * GROUP, GROUP)
            lhs = jnp.concatenate([fetched[g * GROUP + k] for k in range(GROUP)], axis=1)
            rhs = jnp.concatenate(
                [
                    panels[chip * 2, at].reshape(GROUP * BLK, TILE),
                    panels[chip * 2 + 1, at].reshape(GROUP * BLK, TILE),
                ],
                axis=1,
            )
            return total + jnp.dot(lhs, rhs, preferred_element_type=jnp.float32)

        lanes = pl.ds(pl.multiple_of(chip * 2 * TILE, 2 * TILE), 2 * TILE)
        product[:, lanes] = lax.fori_loop(
            0, groups, accumulate, jnp.zeros((acc_cols, 2 * TILE), jnp.float32)
        )

    share = rhs_ref.shape[0]
    spot = (me * share) % TILE
    place = (
        lax.broadcasted_iota(jnp.int32, (share, TILE), 0) + spot
        == lax.broadcasted_iota(jnp.int32, (share, TILE), 1)
    ).astype(jnp.bfloat16)
    placed = lax.dot_general(
        rhs_ref[...], place, (((0,), (0,)), ((), ())), preferred_element_type=jnp.float32
    )
    own_lanes = pl.ds(pl.multiple_of((me * share) // TILE * TILE, TILE), TILE)
    product[:, own_lanes] = product[:, own_lanes] - placed

    chunk = acc_cols // count

    def columns(index):
        return pl.ds(pl.multiple_of(index * chunk, chunk), chunk)

    sum_copies = []
    for t in range(1, count):
        copy = remote(product.at[columns(target(t))], shares.at[t], sum_send.at[t], sum_recv.at[t], rows=target(t))
        copy.start()
        sum_copies.append(copy)
    total = product[columns(me), :]
    for t in range(1, count):
        sum_copies[t - 1].wait_recv()
        total = total + shares[t]
    for load in loads[1:]:
        load.wait()

    def apply(right_rows, matrix):
        return lax.dot_general(
            right_rows, matrix, (((1,), (1,)), ((), ())),
            precision=lax.Precision.HIGHEST, preferred_element_type=jnp.float32,
        )

    half = inverse_one.shape[0]
    residual = -total
    second = apply(residual[:, half:], inverse_two[...])
    reduced = residual[:, :half] - apply(second, coupling[...])
    first = apply(reduced, inverse_one[...])
    for k in range(half // TILE):
        solved[k] = first[:, k * TILE : (k + 1) * TILE]
        solved[half // TILE + k] = second[:, k * TILE : (k + 1) * TILE]

    out_copies = []
    for t in range(1, count):
        to = target(t)
        copy = remote(
            solved.at[(to * share) // TILE], returned.at[me], out_send.at[t], out_recv.at[t], rows=to
        )
        copy.start()
        out_copies.append(copy)
    returned[me] = solved[(me * share) // TILE]
    for copy in out_copies:
        copy.wait_recv()
    turned[...] = returned[...].reshape(acc_cols, TILE).T
    out_ref[...] = turned[pl.ds(pl.multiple_of(spot, share), share), :]

    for copy in row_copies + blk_copies + sum_copies + out_copies:
        copy.wait_send()
    for g in range(groups):
        near(0, side, g).wait_send()
        near(1, side, g).wait_send()
        far(left if g % 2 == 0 else right, g).wait_send()
        for slot, cls in enumerate((side, left, right, opposite)):
            pair(slot, cls, g).wait_send()


def body(
    lower_panels,
    parent_solution,
    parent_rows,
    live_counts,
    front_rhs,
    coupling,
    inverse_one,
    inverse_two,
    plane=PLANE,
):
    count = plane[0] * plane[1]
    groups = count // GROUP
    rows_dev = parent_rows.shape[0]
    columns_dev = parent_solution.shape[1]
    panel_width = inverse_one.shape[0]
    pivots = 2 * panel_width
    classes = pivots // TILE
    lists = parent_rows.reshape(count, BLK)
    owners = lists[:, 0] // rows_dev
    index = jnp.arange(count, dtype=jnp.int32)
    block_of = jnp.sum(
        jnp.where(owners[None, :] == index[:, None], index[None, :], 0), axis=1, dtype=jnp.int32
    )
    rows = (lists % rows_dev)[block_of].reshape(count, 1, BLK)
    position = block_of[:, None] * BLK + jnp.arange(BLK, dtype=jnp.int32)[None, :]
    blocks = lower_panels.reshape(count, BLK, TILE)[block_of]
    blocks = jnp.where((position < live_counts[0])[:, :, None], blocks, jnp.zeros((), blocks.dtype))
    vmem = pl.BlockSpec(memory_space=pltpu.VMEM)
    anywhere = pl.BlockSpec(memory_space=pl.ANY)
    dma = pltpu.SemaphoreType.DMA
    f32, bf16 = jnp.float32, jnp.bfloat16
    return pl.pallas_call(
        functools.partial(kernel, plane),
        out_shape=jax.ShapeDtypeStruct((front_rhs.shape[0], columns_dev), f32),
        in_specs=[vmem, vmem, anywhere, vmem, anywhere, anywhere, anywhere],
        out_specs=vmem,
        scratch_shapes=[
            pltpu.VMEM((classes, count, BLK, TILE), bf16),
            pltpu.VMEM((count, 1, BLK), jnp.int32),
            pltpu.SMEM((count, 1, BLK), jnp.int32),
            pltpu.VMEM((rows_dev, columns_dev), bf16),
            pltpu.VMEM((rows_dev, columns_dev), f32),
            pltpu.VMEM((BLK, columns_dev), f32),
            pltpu.VMEM((count, columns_dev, BLK), bf16),
            pltpu.VMEM((columns_dev, pivots), f32),
            pltpu.VMEM((count, columns_dev // count, pivots), f32),
            pltpu.VMEM((panel_width, panel_width), f32),
            pltpu.VMEM((panel_width, panel_width), f32),
            pltpu.VMEM((panel_width, panel_width), f32),
            pltpu.VMEM((classes, columns_dev // count, TILE), f32),
            pltpu.VMEM((count, columns_dev // count, TILE), f32),
            pltpu.VMEM((TILE, columns_dev), f32),
            dma((4,)),
            dma,
            dma((2,)),
            dma((count,)),
            dma((count,)),
            dma((count,)),
            dma((count,)),
            dma((2, groups)),
            dma((2, groups)),
            dma((groups,)),
            dma((groups,)),
            dma((4, groups)),
            dma((4, groups)),
            dma((count,)),
            dma((count,)),
            dma((count,)),
            dma((count,)),
        ],
        compiler_params=pltpu.CompilerParams(
            collective_id=0, has_side_effects=True, vmem_limit_bytes=48 * 1024 * 1024
        ),
    )(blocks, rows, parent_solution, front_rhs, coupling, inverse_one, inverse_two)


def solution(mesh):
    return jax.shard_map(
        body,
        mesh=mesh,
        in_specs=(
            P("rows", "rhs"),
            P("rows", "rhs"),
            P("rows"),
            P("rows"),
            P("rows", "rhs"),
            P(),
            P(),
            P(),
        ),
        out_specs=P("rows", "rhs"),
        check_vma=False,
    )
```

```python
import functools

import jax
import jax.numpy as jnp
from jax import lax
from jax.experimental import pallas as pl
from jax.experimental.pallas import tpu as pltpu
from jax.sharding import PartitionSpec as P

BLK = 128
TILE = 128
PLANE = (4, 8)
RING = 4
GROUP = 4
MESH = pl.DeviceIdType.MESH


def offsets(plane):
    size_y, size_z = plane
    pairs = [(dy, dz) for dy in range(size_y) for dz in range(size_z)]
    return sorted(
        pairs, key=lambda p: (min(p[1], size_z - p[1]), min(p[0], size_y - p[0]), p)
    )


def split(value):
    high = value.astype(jnp.bfloat16)
    low = (value - high.astype(jnp.float32)).astype(jnp.bfloat16)
    return high, low


def dot_split(left, right):
    def dot(a, b):
        return jnp.dot(a, b, preferred_element_type=jnp.float32)

    return dot(left[0], right[0]) + (dot(left[0], right[1]) + dot(left[1], right[0]))


def kernel(
    plane,
    blocks_ref,
    rows_ref,
    parent_ref,
    rhs_ref,
    coupling_hbm,
    inverse_one_hbm,
    inverse_two_hbm,
    out_ref,
    panels,
    row_buf,
    row_smem,
    staged,
    wide,
    picked,
    fetched,
    product,
    matrices,
    high,
    low,
    first_y,
    first_z,
    second_y,
    second_z,
    got_y,
    got_z,
    got_yz,
    got_zy,
    load_sem,
    smem_sem,
    self_sem,
    row_send,
    row_recv,
    blk_send,
    blk_recv,
    near_send,
    near_recv,
    far_send,
    far_recv,
    twin_send,
    twin_recv,
    y_send,
    y_recv,
    z_send,
    z_recv,
    yz_send,
    yz_recv,
    zy_send,
    zy_recv,
):
    size_y, size_z = plane
    count = size_y * size_z
    groups = count // GROUP
    offs = offsets(plane)
    me = lax.axis_index("rows")
    side = lax.axis_index("rhs")
    y, z = me // size_z, me % size_z
    x, core = side // 2, side % 2
    right = ((x + 1) % RING) * 2 + core
    left = ((x + RING - 1) % RING) * 2 + core
    opposite = ((x + 2) % RING) * 2 + core
    twin = x * 2 + (1 - core)

    def target(t):
        dy, dz = offs[t]
        return ((y + size_y - dy) % size_y) * size_z + (z + size_z - dz) % size_z

    def source(t):
        dy, dz = offs[t]
        return ((y + dy) % size_y) * size_z + (z + dz) % size_z

    def remote(src, dst, send, recv, **device):
        return pltpu.make_async_remote_copy(
            src_ref=src, dst_ref=dst, send_sem=send, recv_sem=recv,
            device_id=device, device_id_type=MESH,
        )

    barrier = pltpu.get_barrier_semaphore()
    for t in range(1, count):
        pl.semaphore_signal(barrier, inc=1, device_id={"rows": target(t)}, device_id_type=MESH)
    for other in (left, right, twin):
        pl.semaphore_signal(barrier, inc=1, device_id={"rhs": other}, device_id_type=MESH)

    loads = [
        pltpu.make_async_copy(parent_ref, staged, load_sem.at[0]),
        pltpu.make_async_copy(coupling_hbm, matrices.at[0], load_sem.at[1]),
        pltpu.make_async_copy(inverse_one_hbm, matrices.at[1], load_sem.at[2]),
        pltpu.make_async_copy(inverse_two_hbm, matrices.at[2], load_sem.at[3]),
    ]
    for load in loads:
        load.start()
    own_block = pltpu.make_async_copy(blocks_ref.at[me], panels.at[side, 0], self_sem.at[0])
    own_block.start()
    own_rows = pltpu.make_async_copy(rows_ref.at[me], row_buf.at[0], self_sem.at[1])
    own_rows.start()

    loads[0].wait()
    depth = staged.shape[0]
    step = 256

    def widen(i, carry):
        at = pl.ds(pl.multiple_of(i * step, step), step)
        wide[at, :] = staged[at, :].astype(jnp.float32)
        return carry

    lax.fori_loop(0, depth // step, widen, 0)
    wide[depth:, :] = jnp.zeros((wide.shape[0] - depth, wide.shape[1]), jnp.float32)

    pl.semaphore_wait(barrier, count + 2)

    row_copies, blk_copies = [], []
    for t in range(1, count):
        copy = remote(rows_ref.at[target(t)], row_buf.at[t], row_send.at[t], row_recv.at[t], rows=target(t))
        copy.start()
        row_copies.append(copy)
    for t in range(1, count):
        copy = remote(
            blocks_ref.at[target(t)], panels.at[side, t], blk_send.at[t], blk_recv.at[t], rows=target(t)
        )
        copy.start()
        blk_copies.append(copy)

    def part(cls, g):
        return panels.at[cls, pl.ds(g * GROUP, GROUP)]

    def near(direction, cls, g):
        other = right if direction == 0 else left
        return remote(part(cls, g), part(cls, g), near_send.at[direction, g], near_recv.at[direction, g], rhs=other)

    def far(cls, g):
        other = right if g % 2 == 0 else left
        return remote(part(cls, g), part(cls, g), far_send.at[g], far_recv.at[g], rhs=other)

    def pair(slot, cls, g):
        return remote(part(cls, g), part(cls, g), twin_send.at[slot, g], twin_recv.at[slot, g], rhs=twin)

    for load in loads[1:]:
        load.wait()
    for k in range(3):
        high[k], low[k] = split(matrices[k])

    own_rows.wait()
    for copy in row_copies:
        copy.wait_recv()
    to_smem = pltpu.make_async_copy(row_buf, row_smem, smem_sem)
    to_smem.start()
    to_smem.wait()

    def gather(t):
        def eight(i, carry):
            for u in range(8):
                at = row_smem[t, 0, i * 8 + u]
                picked[pl.ds(i * 8 + u, 1), :] = wide[pl.ds(at, 1), :]
            return carry

        lax.fori_loop(0, BLK // 8, eight, 0)
        fetched[t] = picked[...].T.astype(jnp.bfloat16)

    def gather_group(g):
        def one(k, carry):
            gather(g * GROUP + k)
            return carry

        lax.fori_loop(0, GROUP, one, 0)

    def from_side(g):
        near(0, left, g).wait_recv()
        if g % 2 == 0:
            far(left, g).start()
        pair(1, left, g).start()
        near(1, right, g).wait_recv()
        if g % 2 == 1:
            far(right, g).start()
        pair(2, right, g).start()

    def from_far(g):
        far(opposite, g).wait_recv()
        pair(3, opposite, g).start()

    for g in range(groups):
        for t in range(g * GROUP, (g + 1) * GROUP):
            if t == 0:
                own_block.wait()
            else:
                blk_copies[t - 1].wait_recv()
        near(0, side, g).start()
        near(1, side, g).start()
        pair(0, side, g).start()
        if g >= 2:
            from_side(g - 2)
        if g >= 5:
            from_far(g - 5)
        gather_group(g)
    for g in range(max(groups - 2, 0), groups):
        from_side(g)

    acc_cols = fetched.shape[1]
    chips = [x, (x + RING - 1) % RING, (x + 1) % RING, (x + 2) % RING]

    def multiply(slot, wait_each):
        chip = chips[slot]
        width = 2 * TILE

        def term(g):
            at = pl.ds(g * GROUP, GROUP)
            lhs = jnp.concatenate([fetched[g * GROUP + k] for k in range(GROUP)], axis=1)
            rhs = jnp.concatenate(
                [panels[chip * 2 + c, at].reshape(GROUP * BLK, TILE) for c in range(2)], axis=1
            )
            return jnp.dot(lhs, rhs, preferred_element_type=jnp.float32)

        if wait_each:
            total = jnp.zeros((acc_cols, width), jnp.float32)
            for g in range(groups):
                pair(slot, chip * 2 + (1 - core), g).wait_recv()
                total = total + term(g)
        else:
            for g in range(groups):
                pair(slot, chip * 2 + (1 - core), g).wait_recv()
            total = lax.fori_loop(
                0, groups, lambda g, s: s + term(g), jnp.zeros((acc_cols, width), jnp.float32)
            )
        product[pl.ds(pl.multiple_of(chip * width, width), width), :] = -total.T

    early = max(groups - 5, 0)
    multiply(0, False)
    for g in range(early, groups - 2):
        from_far(g)
    multiply(1, False)
    multiply(2, False)
    for g in range(max(groups - 2, early), groups):
        from_far(g)
    multiply(3, False)

    share = rhs_ref.shape[0]
    own = pl.ds(pl.multiple_of(me * share, share), share)
    product[own, :] = product[own, :] + rhs_ref[...].astype(jnp.float32)
    half = matrices.shape[1]
    units = share // 8
    stripes = units - 1

    def place(value, base):
        for r in range(half // share):
            index_y, index_z = divmod(base + r, size_z)
            for u in range(units):
                rows = value[r * share + u * 8 : r * share + u * 8 + 8]
                if u < stripes:
                    first_y[u, index_y, index_z] = rows
                else:
                    first_z[index_z, index_y] = rows

    second = dot_split((high[2], low[2]), split(product[half:, :]))
    place(second, half // share)
    reduced = product[:half, :] - dot_split((high[0], low[0]), split(second))
    place(dot_split((high[1], low[1]), split(reduced)), 0)

    y_copies, z_copies, yz_copies, zy_copies = [], [], [], []
    for u in range(stripes):
        for dy in range(1, size_y):
            to = (y + size_y - dy) % size_y
            copy = remote(
                first_y.at[u, to], got_y.at[u, dy - 1], y_send.at[u, dy - 1], y_recv.at[u, dy - 1],
                rows=to * size_z + z,
            )
            copy.start()
            y_copies.append(copy)
        if u == 0:
            for dz in range(1, size_z):
                to = (z + size_z - dz) % size_z
                copy = remote(
                    first_z.at[to], got_z.at[dz - 1], z_send.at[dz - 1], z_recv.at[dz - 1],
                    rows=y * size_z + to,
                )
                copy.start()
                z_copies.append(copy)

    def reduce_y(u):
        total = first_y[u, y]
        for dy in range(1, size_y):
            y_copies[u * (size_y - 1) + dy - 1].wait_recv()
            total = total + got_y[u, dy - 1]
        second_z[u] = total
        for dz in range(1, size_z):
            to = (z + size_z - dz) % size_z
            copy = remote(
                second_z.at[u, to], got_yz.at[u, dz - 1], yz_send.at[u, dz - 1], yz_recv.at[u, dz - 1],
                rows=y * size_z + to,
            )
            copy.start()
            yz_copies.append(copy)

    def reduce_z():
        total = first_z[z]
        for dz in range(1, size_z):
            z_copies[dz - 1].wait_recv()
            total = total + got_z[dz - 1]
        second_y[...] = total
        for dy in range(1, size_y):
            to = (y + size_y - dy) % size_y
            copy = remote(
                second_y.at[to], got_zy.at[dy - 1], zy_send.at[dy - 1], zy_recv.at[dy - 1],
                rows=to * size_z + z,
            )
            copy.start()
            zy_copies.append(copy)

    for u in range(stripes - 1):
        reduce_y(u)
    reduce_z()
    reduce_y(stripes - 1)
    for u in range(stripes):
        total = second_z[u, z]
        for dz in range(1, size_z):
            yz_copies[u * (size_z - 1) + dz - 1].wait_recv()
            total = total + got_yz[u, dz - 1]
        out_ref[u * 8 : u * 8 + 8, :] = total
    total = second_y[y]
    for copy, dy in zip(zy_copies, range(1, size_y)):
        copy.wait_recv()
        total = total + got_zy[dy - 1]
    out_ref[stripes * 8 :, :] = total

    for copy in row_copies + blk_copies + y_copies + z_copies + yz_copies + zy_copies:
        copy.wait_send()
    for g in range(groups):
        near(0, side, g).wait_send()
        near(1, side, g).wait_send()
        far(left if g % 2 == 0 else right, g).wait_send()
        for slot, cls in enumerate((side, left, right, opposite)):
            pair(slot, cls, g).wait_send()


def body(
    lower_panels,
    parent_solution,
    parent_rows,
    live_counts,
    front_rhs,
    coupling,
    inverse_one,
    inverse_two,
    plane=PLANE,
):
    count = plane[0] * plane[1]
    groups = count // GROUP
    rows_dev = parent_rows.shape[0]
    columns_dev = parent_solution.shape[1]
    panel_width = inverse_one.shape[0]
    pivots = 2 * panel_width
    classes = pivots // TILE
    lists = parent_rows.reshape(count, BLK)
    owners = lists[:, 0] // rows_dev
    index = jnp.arange(count, dtype=jnp.int32)
    block_of = jnp.sum(
        jnp.where(owners[None, :] == index[:, None], index[None, :], 0), axis=1, dtype=jnp.int32
    )
    position = block_of[:, None] * BLK + jnp.arange(BLK, dtype=jnp.int32)[None, :]
    rows = jnp.where(position < live_counts[0], (lists % rows_dev)[block_of], rows_dev)
    rows = rows.reshape(count, 1, BLK)
    blocks = lower_panels.reshape(count, BLK, TILE)[block_of]
    units = front_rhs.shape[0] // 8
    vmem = pl.BlockSpec(memory_space=pltpu.VMEM)
    anywhere = pl.BlockSpec(memory_space=pl.ANY)
    dma = pltpu.SemaphoreType.DMA
    f32, bf16 = jnp.float32, jnp.bfloat16
    return pl.pallas_call(
        functools.partial(kernel, plane),
        out_shape=jax.ShapeDtypeStruct((front_rhs.shape[0], columns_dev), f32),
        in_specs=[vmem, vmem, anywhere, vmem, anywhere, anywhere, anywhere],
        out_specs=vmem,
        scratch_shapes=[
            pltpu.VMEM((classes, count, BLK, TILE), bf16),
            pltpu.VMEM((count, 1, BLK), jnp.int32),
            pltpu.SMEM((count, 1, BLK), jnp.int32),
            pltpu.VMEM((rows_dev, columns_dev), bf16),
            pltpu.VMEM((rows_dev + 8, columns_dev), f32),
            pltpu.VMEM((BLK, columns_dev), f32),
            pltpu.VMEM((count, columns_dev, BLK), bf16),
            pltpu.VMEM((pivots, columns_dev), f32),
            pltpu.VMEM((3, panel_width, panel_width), f32),
            pltpu.VMEM((3, panel_width, panel_width), bf16),
            pltpu.VMEM((3, panel_width, panel_width), bf16),
            pltpu.VMEM((units - 1, plane[0], plane[1], 8, columns_dev), f32),
            pltpu.VMEM((plane[1], plane[0], 8, columns_dev), f32),
            pltpu.VMEM((plane[0], 8, columns_dev), f32),
            pltpu.VMEM((units - 1, plane[1], 8, columns_dev), f32),
            pltpu.VMEM((units - 1, plane[0] - 1, plane[1], 8, columns_dev), f32),
            pltpu.VMEM((plane[1] - 1, plane[0], 8, columns_dev), f32),
            pltpu.VMEM((units - 1, plane[1] - 1, 8, columns_dev), f32),
            pltpu.VMEM((plane[0] - 1, 8, columns_dev), f32),
            dma((4,)),
            dma,
            dma((2,)),
            dma((count,)),
            dma((count,)),
            dma((count,)),
            dma((count,)),
            dma((2, groups)),
            dma((2, groups)),
            dma((groups,)),
            dma((groups,)),
            dma((4, groups)),
            dma((4, groups)),
            dma((units - 1, plane[0] - 1)),
            dma((units - 1, plane[0] - 1)),
            dma((plane[1] - 1,)),
            dma((plane[1] - 1,)),
            dma((units - 1, plane[1] - 1)),
            dma((units - 1, plane[1] - 1)),
            dma((plane[0] - 1,)),
            dma((plane[0] - 1,)),
        ],
        compiler_params=pltpu.CompilerParams(
            collective_id=0, has_side_effects=True, vmem_limit_bytes=48 * 1024 * 1024
        ),
    )(blocks, rows, parent_solution, front_rhs, coupling, inverse_one, inverse_two)


def solution(mesh):
    return jax.shard_map(
        body,
        mesh=mesh,
        in_specs=(
            P("rows", "rhs"),
            P("rows", "rhs"),
            P("rows"),
            P("rows"),
            P("rows", "rhs"),
            P(),
            P(),
            P(),
        ),
        out_specs=P("rows", "rhs"),
        check_vma=False,
    )
```

```python
import functools

import jax
import jax.numpy as jnp
from jax import lax
from jax.experimental import pallas as pl
from jax.experimental.pallas import tpu as pltpu
from jax.sharding import PartitionSpec as P

BLK = 128
TILE = 128
PLANE = (4, 8)
RING = 4
GROUP = 4
MESH = pl.DeviceIdType.MESH


def offsets(plane):
    size_y, size_z = plane
    pairs = [(dy, dz) for dy in range(size_y) for dz in range(size_z)]
    return sorted(
        pairs, key=lambda p: (min(p[1], size_z - p[1]), min(p[0], size_y - p[0]), p)
    )


def split(value):
    high = value.astype(jnp.bfloat16)
    low = (value - high.astype(jnp.float32)).astype(jnp.bfloat16)
    return high, low


def dot_split(left, right):
    def dot(a, b):
        return jnp.dot(a, b, preferred_element_type=jnp.float32)

    return dot(left[0], right[0]) + (dot(left[0], right[1]) + dot(left[1], right[0]))


def kernel(
    plane,
    live_ref,
    lists_ref,
    lower_hbm,
    parent_ref,
    rhs_ref,
    coupling_hbm,
    inverse_one_hbm,
    inverse_two_hbm,
    out_ref,
    order_buf,
    order_ref,
    held,
    blocks_ref,
    rows_ref,
    panels,
    row_buf,
    row_smem,
    staged,
    wide,
    picked,
    fetched,
    product,
    partial,
    matrices,
    high,
    low,
    first_y,
    first_z,
    second_y,
    second_z,
    got_y,
    got_z,
    got_yz,
    got_zy,
    load_sem,
    smem_sem,
    row_send,
    row_recv,
    blk_send,
    blk_recv,
    near_send,
    near_recv,
    far_send,
    far_recv,
    twin_send,
    twin_recv,
    y_send,
    y_recv,
    z_send,
    z_recv,
    yz_send,
    yz_recv,
    zy_send,
    zy_recv,
):
    size_y, size_z = plane
    count = size_y * size_z
    groups = count // GROUP
    offs = offsets(plane)
    me = lax.axis_index("rows")
    side = lax.axis_index("rhs")
    y, z = me // size_z, me % size_z
    x, core = side // 2, side % 2
    right = ((x + 1) % RING) * 2 + core
    left = ((x + RING - 1) % RING) * 2 + core
    opposite = ((x + 2) % RING) * 2 + core
    twin = x * 2 + (1 - core)

    def target(t):
        dy, dz = offs[t]
        return ((y + size_y - dy) % size_y) * size_z + (z + size_z - dz) % size_z

    def source(t):
        dy, dz = offs[t]
        return ((y + dy) % size_y) * size_z + (z + dz) % size_z

    def remote(src, dst, send, recv, **device):
        return pltpu.make_async_remote_copy(
            src_ref=src, dst_ref=dst, send_sem=send, recv_sem=recv,
            device_id=device, device_id_type=MESH,
        )

    barrier = pltpu.get_barrier_semaphore()
    for t in range(1, count):
        pl.semaphore_signal(barrier, inc=1, device_id={"rows": target(t)}, device_id_type=MESH)
    for other in (left, right, twin):
        pl.semaphore_signal(barrier, inc=1, device_id={"rhs": other}, device_id_type=MESH)

    loads = [
        pltpu.make_async_copy(parent_ref, staged, load_sem.at[0]),
        pltpu.make_async_copy(coupling_hbm, matrices.at[0], load_sem.at[1]),
        pltpu.make_async_copy(inverse_one_hbm, matrices.at[1], load_sem.at[2]),
        pltpu.make_async_copy(inverse_two_hbm, matrices.at[2], load_sem.at[3]),
        pltpu.make_async_copy(lower_hbm, held, load_sem.at[4]),
    ]
    loads[4].start()
    for load in loads[:4]:
        load.start()
    rows_dev = staged.shape[0]
    lane = lax.broadcasted_iota(jnp.int32, (1, BLK), 1)
    owner = lax.div(lists_ref[:, 0:1], jnp.int32(rows_dev))
    number = lax.broadcasted_iota(jnp.int32, (count, BLK), 0)
    order_buf[...] = jnp.max(jnp.where(owner == lane, number, 0), axis=0, keepdims=True)
    to_order = pltpu.make_async_copy(order_buf, order_ref, smem_sem.at[1])
    to_order.start()
    to_order.wait()
    loads[4].wait()

    def arrange(index, carry):
        block = order_ref[0, index]
        blocks_ref[index] = held[block]
        alive = lane + block * BLK < live_ref[0]
        local = lax.rem(lists_ref[pl.ds(block, 1), :], jnp.int32(rows_dev))
        rows_ref[index] = jnp.where(alive, local, rows_dev)
        return carry

    lax.fori_loop(0, count, arrange, 0)
    panels[side, 0] = blocks_ref[me]
    row_buf[0] = rows_ref[me]

    loads[0].wait()
    depth = staged.shape[0]
    step = 256

    def widen(i, carry):
        at = pl.ds(pl.multiple_of(i * step, step), step)
        wide[at, :] = staged[at, :].astype(jnp.float32)
        return carry

    lax.fori_loop(0, depth // step, widen, 0)
    wide[depth:, :] = jnp.zeros((wide.shape[0] - depth, wide.shape[1]), jnp.float32)

    pl.semaphore_wait(barrier, count + 2)

    row_copies, blk_copies = [], []
    for t in range(1, count):
        copy = remote(rows_ref.at[target(t)], row_buf.at[t], row_send.at[t], row_recv.at[t], rows=target(t))
        copy.start()
        row_copies.append(copy)
    for t in range(1, count):
        copy = remote(
            blocks_ref.at[target(t)], panels.at[side, t], blk_send.at[t], blk_recv.at[t], rows=target(t)
        )
        copy.start()
        blk_copies.append(copy)

    def part(cls, g):
        return panels.at[cls, pl.ds(g * GROUP, GROUP)]

    def near(direction, cls, g):
        other = right if direction == 0 else left
        return remote(part(cls, g), part(cls, g), near_send.at[direction, g], near_recv.at[direction, g], rhs=other)

    def far(cls, g):
        other = right if g % 2 == 0 else left
        return remote(part(cls, g), part(cls, g), far_send.at[g], far_recv.at[g], rhs=other)

    def pair(slot, cls, g):
        return remote(part(cls, g), part(cls, g), twin_send.at[slot, g], twin_recv.at[slot, g], rhs=twin)

    def take_rows():
        for copy in row_copies:
            copy.wait_recv()
        to_smem = pltpu.make_async_copy(row_buf, row_smem, smem_sem.at[0])
        to_smem.start()
        to_smem.wait()

    def gather(t):
        def eight(i, carry):
            for u in range(8):
                at = row_smem[t, 0, i * 8 + u]
                picked[pl.ds(i * 8 + u, 1), :] = wide[pl.ds(at, 1), :]
            return carry

        lax.fori_loop(0, BLK // 8, eight, 0)
        fetched[t] = picked[...].T.astype(jnp.bfloat16)

    def gather_group(g):
        def one(k, carry):
            gather(g * GROUP + k)
            return carry

        lax.fori_loop(0, GROUP, one, 0)

    acc_cols = fetched.shape[1]
    width = 2 * TILE
    chips = [x, (x + RING - 1) % RING, (x + 1) % RING, (x + 2) % RING]
    half = matrices.shape[1]

    def forward(g):
        for t in range(g * GROUP, (g + 1) * GROUP):
            if t > 0:
                blk_copies[t - 1].wait_recv()
        near(0, side, g).start()
        near(1, side, g).start()
        pair(0, side, g).start()

    def from_side(g):
        near(0, left, g).wait_recv()
        pair(1, left, g).start()
        near(1, right, g).wait_recv()
        pair(2, right, g).start()

    def relay(g):
        far(left if g % 2 == 0 else right, g).start()

    def from_far(g):
        far(opposite, g).wait_recv()
        pair(3, opposite, g).start()

    def term(slot, g):
        chip = chips[slot]
        pair(slot, chip * 2 + (1 - core), g).wait_recv()
        at = pl.ds(g * GROUP, GROUP)
        lhs = jnp.concatenate([fetched[g * GROUP + k] for k in range(GROUP)], axis=1)
        rhs = jnp.concatenate(
            [panels[chip * 2 + c, at].reshape(GROUP * BLK, TILE) for c in range(2)], axis=1
        )
        value = jnp.dot(lhs, rhs, preferred_element_type=jnp.float32)
        partial[slot] = value if g == 0 else partial[slot] + value

    def put(rows, columns, value):
        top, bottom = split(value)
        high[rows, columns] = top
        low[rows, columns] = bottom

    upper, lower = slice(0, half), slice(half, 2 * half)

    def invert(stage):
        if stage == 0:
            for load in loads[1:4]:
                load.wait()
            put(upper, upper, matrices[1])
            put(lower, lower, matrices[2])
            put(lower, upper, matrices[0])
        if stage == 1:
            put(upper, lower, dot_split(
                (high[lower, upper], low[lower, upper]), (high[lower, lower], low[lower, lower])
            ))
        if stage == 2:
            put(upper, lower, -dot_split(
                (high[upper, upper], low[upper, upper]), (high[upper, lower], low[upper, lower])
            ))
            high[lower, upper] = jnp.zeros((half, half), jnp.bfloat16)
            low[lower, upper] = jnp.zeros((half, half), jnp.bfloat16)

    for g in range(groups + 4):
        if g == groups - 1:
            relay(0)
            relay(1)
        if g < groups:
            forward(g)
        if g == 1:
            take_rows()
        if 2 <= g < groups + 2:
            from_side(g - 2)
        if g >= groups:
            for k in range(2 if g == groups else groups - 2 if g == groups + 1 else groups,
                           groups - 2 if g == groups else groups if g == groups + 1 else groups):
                relay(k)
        if 1 <= g <= groups:
            gather_group(g - 1)
        if g == groups - 4:
            invert(0)
        if g == groups - 3:
            invert(1)
        if g == groups - 2:
            invert(2)
        if 3 <= g < groups + 3:
            term(0, g - 3)
        if g >= 4:
            term(1, g - 4)
            term(2, g - 4)

    def pivots(slot):
        return pl.ds(pl.multiple_of(chips[slot] * width, width), width)

    for g in range(groups // 2):
        from_far(g)
    share = rhs_ref.shape[0]
    own = pl.ds(pl.multiple_of(me * share, share), share)
    for slot in range(3):
        product[pivots(slot), :] = -partial[slot].T
    product[pivots(3), :] = jnp.zeros((width, acc_cols), jnp.float32)
    product[own, :] = product[own, :] + rhs_ref[...].astype(jnp.float32)
    product[...] = dot_split((high[...], low[...]), split(product[...]))
    for g in range(groups // 2):
        term(3, g)
    for g in range(groups // 2, groups):
        from_far(g)
        if g > groups // 2:
            term(3, g - 1)
    term(3, groups - 1)

    units = share // 8
    stripes = units - 1
    last = dot_split((high[:, pivots(3)], low[:, pivots(3)]), split(-partial[3].T))
    answer = product[...] + last
    for r in range(count):
        index_y, index_z = divmod(r, size_z)
        for u in range(units):
            rows = answer[r * share + u * 8 : r * share + u * 8 + 8]
            if u < stripes:
                first_y[u, index_y, index_z] = rows
            else:
                first_z[index_z, index_y] = rows

    y_copies, z_copies, yz_copies, zy_copies = [], [], [], []
    for u in range(stripes):
        for dy in range(1, size_y):
            to = (y + size_y - dy) % size_y
            copy = remote(
                first_y.at[u, to], got_y.at[u, dy - 1], y_send.at[u, dy - 1], y_recv.at[u, dy - 1],
                rows=to * size_z + z,
            )
            copy.start()
            y_copies.append(copy)
        if u == 0:
            for dz in range(1, size_z):
                to = (z + size_z - dz) % size_z
                copy = remote(
                    first_z.at[to], got_z.at[dz - 1], z_send.at[dz - 1], z_recv.at[dz - 1],
                    rows=y * size_z + to,
                )
                copy.start()
                z_copies.append(copy)

    def reduce_y(u):
        total = first_y[u, y]
        for dy in range(1, size_y):
            y_copies[u * (size_y - 1) + dy - 1].wait_recv()
            total = total + got_y[u, dy - 1]
        second_z[u] = total
        for dz in range(1, size_z):
            to = (z + size_z - dz) % size_z
            copy = remote(
                second_z.at[u, to], got_yz.at[u, dz - 1], yz_send.at[u, dz - 1], yz_recv.at[u, dz - 1],
                rows=y * size_z + to,
            )
            copy.start()
            yz_copies.append(copy)

    def reduce_z():
        total = first_z[z]
        for dz in range(1, size_z):
            z_copies[dz - 1].wait_recv()
            total = total + got_z[dz - 1]
        second_y[...] = total
        for dy in range(1, size_y):
            to = (y + size_y - dy) % size_y
            copy = remote(
                second_y.at[to], got_zy.at[dy - 1], zy_send.at[dy - 1], zy_recv.at[dy - 1],
                rows=to * size_z + z,
            )
            copy.start()
            zy_copies.append(copy)

    for u in range(stripes - 1):
        reduce_y(u)
    reduce_z()
    reduce_y(stripes - 1)
    for u in range(stripes):
        total = second_z[u, z]
        for dz in range(1, size_z):
            yz_copies[u * (size_z - 1) + dz - 1].wait_recv()
            total = total + got_yz[u, dz - 1]
        out_ref[u * 8 : u * 8 + 8, :] = total
    total = second_y[y]
    for copy, dy in zip(zy_copies, range(1, size_y)):
        copy.wait_recv()
        total = total + got_zy[dy - 1]
    out_ref[stripes * 8 :, :] = total

    for copy in row_copies + blk_copies + y_copies + z_copies + yz_copies + zy_copies:
        copy.wait_send()
    for g in range(groups):
        near(0, side, g).wait_send()
        near(1, side, g).wait_send()
        far(left if g % 2 == 0 else right, g).wait_send()
        for slot, cls in enumerate((side, left, right, opposite)):
            pair(slot, cls, g).wait_send()


def body(
    lower_panels,
    parent_solution,
    parent_rows,
    live_counts,
    front_rhs,
    coupling,
    inverse_one,
    inverse_two,
    plane=PLANE,
):
    count = plane[0] * plane[1]
    groups = count // GROUP
    rows_dev = parent_rows.shape[0]
    columns_dev = parent_solution.shape[1]
    panel_width = inverse_one.shape[0]
    pivots = 2 * panel_width
    classes = pivots // TILE
    units = front_rhs.shape[0] // 8
    vmem = pl.BlockSpec(memory_space=pltpu.VMEM)
    smem = pl.BlockSpec(memory_space=pltpu.SMEM)
    hbm = pl.BlockSpec(memory_space=pltpu.HBM)
    dma = pltpu.SemaphoreType.DMA
    f32, bf16 = jnp.float32, jnp.bfloat16
    return pl.pallas_call(
        functools.partial(kernel, plane),
        out_shape=jax.ShapeDtypeStruct((front_rhs.shape[0], columns_dev), f32),
        in_specs=[smem, vmem, hbm, hbm, vmem, hbm, hbm, hbm],
        out_specs=vmem,
        scratch_shapes=[
            pltpu.VMEM((1, BLK), jnp.int32),
            pltpu.SMEM((1, BLK), jnp.int32),
            pltpu.VMEM((count, BLK, TILE), bf16),
            pltpu.VMEM((count, BLK, TILE), bf16),
            pltpu.VMEM((count, 1, BLK), jnp.int32),
            pltpu.VMEM((classes, count, BLK, TILE), bf16),
            pltpu.VMEM((count, 1, BLK), jnp.int32),
            pltpu.SMEM((count, 1, BLK), jnp.int32),
            pltpu.VMEM((rows_dev, columns_dev), bf16),
            pltpu.VMEM((rows_dev + 8, columns_dev), f32),
            pltpu.VMEM((BLK, columns_dev), f32),
            pltpu.VMEM((count, columns_dev, BLK), bf16),
            pltpu.VMEM((pivots, columns_dev), f32),
            pltpu.VMEM((4, columns_dev, 2 * TILE), f32),
            pltpu.VMEM((3, panel_width, panel_width), f32),
            pltpu.VMEM((pivots, pivots), bf16),
            pltpu.VMEM((pivots, pivots), bf16),
            pltpu.VMEM((units - 1, plane[0], plane[1], 8, columns_dev), f32),
            pltpu.VMEM((plane[1], plane[0], 8, columns_dev), f32),
            pltpu.VMEM((plane[0], 8, columns_dev), f32),
            pltpu.VMEM((units - 1, plane[1], 8, columns_dev), f32),
            pltpu.VMEM((units - 1, plane[0] - 1, plane[1], 8, columns_dev), f32),
            pltpu.VMEM((plane[1] - 1, plane[0], 8, columns_dev), f32),
            pltpu.VMEM((units - 1, plane[1] - 1, 8, columns_dev), f32),
            pltpu.VMEM((plane[0] - 1, 8, columns_dev), f32),
            dma((5,)),
            dma((2,)),
            dma((count,)),
            dma((count,)),
            dma((count,)),
            dma((count,)),
            dma((2, groups)),
            dma((2, groups)),
            dma((groups,)),
            dma((groups,)),
            dma((4, groups)),
            dma((4, groups)),
            dma((units - 1, plane[0] - 1)),
            dma((units - 1, plane[0] - 1)),
            dma((plane[1] - 1,)),
            dma((plane[1] - 1,)),
            dma((units - 1, plane[1] - 1)),
            dma((units - 1, plane[1] - 1)),
            dma((plane[0] - 1,)),
            dma((plane[0] - 1,)),
        ],
        compiler_params=pltpu.CompilerParams(
            collective_id=0, has_side_effects=True, vmem_limit_bytes=67043328
        ),
    )(
        live_counts,
        parent_rows.reshape(count, BLK),
        lower_panels.reshape(count, BLK, TILE),
        parent_solution,
        front_rhs,
        coupling,
        inverse_one,
        inverse_two,
    )


def solution(mesh):
    return jax.shard_map(
        body,
        mesh=mesh,
        in_specs=(
            P("rows", "rhs"),
            P("rows", "rhs"),
            P("rows"),
            P("rows"),
            P("rows", "rhs"),
            P(),
            P(),
            P(),
        ),
        out_specs=P("rows", "rhs"),
        check_vma=False,
    )
```

```python
import functools

import jax
import jax.numpy as jnp
from jax import lax
from jax.experimental import pallas as pl
from jax.experimental.pallas import tpu as pltpu
from jax.sharding import PartitionSpec as P

BLK = 128
TILE = 128
PLANE = (4, 8)
RING = 4
GROUP = 4
BATCH = 2
AHEAD = 2
VMEM_BYTES = 66781184
MESH = pl.DeviceIdType.MESH


def offsets(plane):
    size_y, size_z = plane
    pairs = [(dy, dz) for dy in range(size_y) for dz in range(size_z)]
    return sorted(
        pairs, key=lambda p: (min(p[1], size_z - p[1]), min(p[0], size_y - p[0]), p)
    )


def split(value):
    high = value.astype(jnp.bfloat16)
    low = (value - high.astype(jnp.float32)).astype(jnp.bfloat16)
    return high, low


def dot_split(left, right):
    def dot(a, b):
        return jnp.dot(a, b, preferred_element_type=jnp.float32)

    return dot(left[0], right[0]) + (dot(left[0], right[1]) + dot(left[1], right[0]))


def kernel(
    plane,
    live_ref,
    lists_ref,
    lower_hbm,
    parent_ref,
    rhs_ref,
    coupling_hbm,
    inverse_one_hbm,
    inverse_two_hbm,
    out_ref,
    order_buf,
    order_ref,
    held,
    blocks_ref,
    rows_ref,
    panels,
    row_buf,
    row_smem,
    staged,
    wide,
    picked,
    fetched,
    product,
    partial,
    matrices,
    high,
    low,
    first_y,
    first_z,
    second_y,
    second_z,
    got_y,
    got_z,
    got_yz,
    got_zy,
    load_sem,
    smem_sem,
    row_send,
    row_recv,
    blk_send,
    blk_recv,
    near_send,
    near_recv,
    far_send,
    far_recv,
    twin_send,
    twin_recv,
    y_send,
    y_recv,
    z_send,
    z_recv,
    yz_send,
    yz_recv,
    zy_send,
    zy_recv,
):
    size_y, size_z = plane
    count = size_y * size_z
    groups = count // GROUP
    offs = offsets(plane)
    me = lax.axis_index("rows")
    side = lax.axis_index("rhs")
    y, z = me // size_z, me % size_z
    x, core = side // 2, side % 2
    right = ((x + 1) % RING) * 2 + core
    left = ((x + RING - 1) % RING) * 2 + core
    opposite = ((x + 2) % RING) * 2 + core
    twin = x * 2 + (1 - core)

    def target(t):
        dy, dz = offs[t]
        return ((y + size_y - dy) % size_y) * size_z + (z + size_z - dz) % size_z

    def source(t):
        dy, dz = offs[t]
        return ((y + dy) % size_y) * size_z + (z + dz) % size_z

    def remote(src, dst, send, recv, **device):
        return pltpu.make_async_remote_copy(
            src_ref=src, dst_ref=dst, send_sem=send, recv_sem=recv,
            device_id=device, device_id_type=MESH,
        )

    barrier = pltpu.get_barrier_semaphore()
    for t in range(1, count):
        pl.semaphore_signal(barrier, inc=1, device_id={"rows": target(t)}, device_id_type=MESH)
    for other in (left, right, twin):
        pl.semaphore_signal(barrier, inc=1, device_id={"rhs": other}, device_id_type=MESH)

    loads = [
        pltpu.make_async_copy(parent_ref, staged, load_sem.at[0]),
        pltpu.make_async_copy(coupling_hbm, matrices.at[0], load_sem.at[1]),
        pltpu.make_async_copy(inverse_one_hbm, matrices.at[1], load_sem.at[2]),
        pltpu.make_async_copy(inverse_two_hbm, matrices.at[2], load_sem.at[3]),
        pltpu.make_async_copy(lower_hbm, held, load_sem.at[4]),
    ]
    loads[4].start()
    for load in loads[:4]:
        load.start()
    rows_dev = staged.shape[0]
    lane = lax.broadcasted_iota(jnp.int32, (1, BLK), 1)
    owner = lax.div(lists_ref[:, 0:1], jnp.int32(rows_dev))
    number = lax.broadcasted_iota(jnp.int32, (count, BLK), 0)
    order_buf[...] = jnp.max(jnp.where(owner == lane, number, 0), axis=0, keepdims=True)
    to_order = pltpu.make_async_copy(order_buf, order_ref, smem_sem.at[1])
    to_order.start()
    to_order.wait()
    loads[4].wait()

    def arrange(index, carry):
        block = order_ref[0, index]
        blocks_ref[index] = held[block]
        alive = lane + block * BLK < live_ref[0]
        local = lax.rem(lists_ref[pl.ds(block, 1), :], jnp.int32(rows_dev))
        rows_ref[index] = jnp.where(alive, local, rows_dev)
        return carry

    lax.fori_loop(0, count, arrange, 0)
    panels[side, 0] = blocks_ref[me]
    row_buf[0] = rows_ref[me]

    pl.semaphore_wait(barrier, count + 2)

    row_copies, blk_copies = [], []
    for t in range(1, count):
        copy = remote(rows_ref.at[target(t)], row_buf.at[t], row_send.at[t], row_recv.at[t], rows=target(t))
        copy.start()
        row_copies.append(copy)
    for t in range(1, count):
        copy = remote(
            blocks_ref.at[target(t)], panels.at[side, t], blk_send.at[t], blk_recv.at[t], rows=target(t)
        )
        copy.start()
        blk_copies.append(copy)

    loads[0].wait()
    depth = staged.shape[0]
    step = 256

    def widen(i, carry):
        at = pl.ds(pl.multiple_of(i * step, step), step)
        wide[at, :] = staged[at, :].astype(jnp.float32)
        return carry

    lax.fori_loop(0, depth // step, widen, 0)
    wide[depth:, :] = jnp.zeros((wide.shape[0] - depth, wide.shape[1]), jnp.float32)

    def part(cls, g):
        return panels.at[cls, pl.ds(g * GROUP, GROUP)]

    def near(direction, cls, g):
        other = right if direction == 0 else left
        return remote(part(cls, g), part(cls, g), near_send.at[direction, g], near_recv.at[direction, g], rhs=other)

    def far(cls, g):
        other = right if g % 2 == 0 else left
        return remote(part(cls, g), part(cls, g), far_send.at[g], far_recv.at[g], rhs=other)

    def batch(cls, b):
        return panels.at[cls, pl.ds(b * BATCH * GROUP, BATCH * GROUP)]

    def pair(slot, cls, b):
        return remote(batch(cls, b), batch(cls, b), twin_send.at[slot, b], twin_recv.at[slot, b], rhs=twin)

    def share_twin(slot, cls, g):
        if (g + 1) % BATCH == 0:
            pair(slot, cls, g // BATCH).start()

    def take_rows():
        for copy in row_copies:
            copy.wait_recv()
        to_smem = pltpu.make_async_copy(row_buf, row_smem, smem_sem.at[0])
        to_smem.start()
        to_smem.wait()

    def gather(t):
        def eight(i, carry):
            for u in range(8):
                at = row_smem[t, 0, i * 8 + u]
                picked[pl.ds(i * 8 + u, 1), :] = wide[pl.ds(at, 1), :]
            return carry

        lax.fori_loop(0, BLK // 8, eight, 0)
        fetched[t] = picked[...].T.astype(jnp.bfloat16)

    def gather_group(g):
        def one(k, carry):
            gather(g * GROUP + k)
            return carry

        lax.fori_loop(0, GROUP, one, 0)

    acc_cols = fetched.shape[1]
    width = 2 * TILE
    chips = [x, (x + RING - 1) % RING, (x + 1) % RING, (x + 2) % RING]
    half = matrices.shape[1]

    def forward(g):
        for t in range(g * GROUP, (g + 1) * GROUP):
            if t > 0:
                blk_copies[t - 1].wait_recv()
        near(0, side, g).start()
        near(1, side, g).start()
        share_twin(0, side, g)

    def from_side(g):
        near(0, left, g).wait_recv()
        share_twin(1, left, g)
        near(1, right, g).wait_recv()
        share_twin(2, right, g)

    def relay(g):
        far(left if g % 2 == 0 else right, g).start()

    def from_far(g):
        far(opposite, g).wait_recv()
        share_twin(3, opposite, g)

    def term(slot, b):
        chip = chips[slot]
        pair(slot, chip * 2 + (1 - core), b).wait_recv()
        size = BATCH * GROUP
        at = pl.ds(b * size, size)
        lhs = jnp.concatenate([fetched[b * size + k] for k in range(size)], axis=1)
        rhs = jnp.concatenate(
            [panels[chip * 2 + c, at].reshape(size * BLK, TILE) for c in range(2)], axis=1
        )
        value = jnp.dot(lhs, rhs, preferred_element_type=jnp.float32)
        partial[slot] = value if b == 0 else partial[slot] + value

    def put(rows, columns, value):
        top, bottom = split(value)
        high[rows, columns] = top
        low[rows, columns] = bottom

    upper, lower = slice(0, half), slice(half, 2 * half)

    def invert(stage):
        if stage == 0:
            for load in loads[1:4]:
                load.wait()
            put(upper, upper, matrices[1])
            put(lower, lower, matrices[2])
            put(lower, upper, matrices[0])
        if stage == 1:
            put(upper, lower, dot_split(
                (high[lower, upper], low[lower, upper]), (high[lower, lower], low[lower, lower])
            ))
        if stage == 2:
            put(upper, lower, -dot_split(
                (high[upper, upper], low[upper, upper]), (high[upper, lower], low[upper, lower])
            ))
            high[lower, upper] = jnp.zeros((half, half), jnp.bfloat16)
            low[lower, upper] = jnp.zeros((half, half), jnp.bfloat16)

    ahead = min(AHEAD, groups - 3)
    for g in range(groups + 4):
        if g == groups - 1:
            for k in range(ahead):
                relay(k)
        if g < groups:
            forward(g)
        if g == 1:
            take_rows()
        if 2 <= g < groups + 2:
            from_side(g - 2)
        if g == groups:
            for k in range(ahead, groups - 1):
                relay(k)
        if g == groups + 1:
            relay(groups - 1)
        if 1 <= g <= groups:
            gather_group(g - 1)
        if g == groups - 4:
            invert(0)
        if g == groups - 3:
            invert(1)
        if g == groups - 2:
            invert(2)
        if 3 <= g < groups + 3 and (g - 2) % BATCH == 0:
            term(0, (g - 3) // BATCH)
        if g >= 4 and (g - 3) % BATCH == 0:
            term(1, (g - 4) // BATCH)
            term(2, (g - 4) // BATCH)

    def pivots(slot):
        return pl.ds(pl.multiple_of(chips[slot] * width, width), width)

    for g in range(groups // 2):
        from_far(g)
    share = rhs_ref.shape[0]
    own = pl.ds(pl.multiple_of(me * share, share), share)
    for slot in range(3):
        product[pivots(slot), :] = -partial[slot].T
    product[pivots(3), :] = jnp.zeros((width, acc_cols), jnp.float32)
    product[own, :] = product[own, :] + rhs_ref[...].astype(jnp.float32)
    product[...] = dot_split((high[...], low[...]), split(product[...]))
    batches = groups // BATCH
    for b in range(batches // 2):
        term(3, b)
    for g in range(groups // 2, groups):
        from_far(g)
        if g >= groups // 2 + BATCH and g % BATCH == BATCH - 1:
            term(3, g // BATCH - 1)
    term(3, batches - 1)

    units = share // 8
    stripes = units - 1
    last = dot_split((high[:, pivots(3)], low[:, pivots(3)]), split(-partial[3].T))
    answer = product[...] + last
    for r in range(count):
        index_y, index_z = divmod(r, size_z)
        for u in range(units):
            rows = answer[r * share + u * 8 : r * share + u * 8 + 8]
            if u < stripes:
                first_y[u, index_y, index_z] = rows
            else:
                first_z[index_z, index_y] = rows

    y_copies, z_copies, yz_copies, zy_copies = [], [], [], []
    for u in range(stripes):
        for dy in range(1, size_y):
            to = (y + size_y - dy) % size_y
            copy = remote(
                first_y.at[u, to], got_y.at[u, dy - 1], y_send.at[u, dy - 1], y_recv.at[u, dy - 1],
                rows=to * size_z + z,
            )
            copy.start()
            y_copies.append(copy)
        if u == 0:
            for dz in range(1, size_z):
                to = (z + size_z - dz) % size_z
                copy = remote(
                    first_z.at[to], got_z.at[dz - 1], z_send.at[dz - 1], z_recv.at[dz - 1],
                    rows=y * size_z + to,
                )
                copy.start()
                z_copies.append(copy)

    def reduce_y(u):
        total = first_y[u, y]
        for dy in range(1, size_y):
            y_copies[u * (size_y - 1) + dy - 1].wait_recv()
            total = total + got_y[u, dy - 1]
        second_z[u] = total
        for dz in range(1, size_z):
            to = (z + size_z - dz) % size_z
            copy = remote(
                second_z.at[u, to], got_yz.at[u, dz - 1], yz_send.at[u, dz - 1], yz_recv.at[u, dz - 1],
                rows=y * size_z + to,
            )
            copy.start()
            yz_copies.append(copy)

    def reduce_z():
        total = first_z[z]
        for dz in range(1, size_z):
            z_copies[dz - 1].wait_recv()
            total = total + got_z[dz - 1]
        second_y[...] = total
        for dy in range(1, size_y):
            to = (y + size_y - dy) % size_y
            copy = remote(
                second_y.at[to], got_zy.at[dy - 1], zy_send.at[dy - 1], zy_recv.at[dy - 1],
                rows=to * size_z + z,
            )
            copy.start()
            zy_copies.append(copy)

    for u in range(stripes - 1):
        reduce_y(u)
    reduce_z()
    reduce_y(stripes - 1)
    for u in range(stripes):
        total = second_z[u, z]
        for dz in range(1, size_z):
            yz_copies[u * (size_z - 1) + dz - 1].wait_recv()
            total = total + got_yz[u, dz - 1]
        out_ref[u * 8 : u * 8 + 8, :] = total
    total = second_y[y]
    for copy, dy in zip(zy_copies, range(1, size_y)):
        copy.wait_recv()
        total = total + got_zy[dy - 1]
    out_ref[stripes * 8 :, :] = total

    for copy in row_copies + blk_copies + y_copies + z_copies + yz_copies + zy_copies:
        copy.wait_send()
    for g in range(groups):
        near(0, side, g).wait_send()
        near(1, side, g).wait_send()
        far(left if g % 2 == 0 else right, g).wait_send()
    for slot, cls in enumerate((side, left, right, opposite)):
        for b in range(batches):
            pair(slot, cls, b).wait_send()


def body(
    lower_panels,
    parent_solution,
    parent_rows,
    live_counts,
    front_rhs,
    coupling,
    inverse_one,
    inverse_two,
    plane=PLANE,
):
    count = plane[0] * plane[1]
    groups = count // GROUP
    rows_dev = parent_rows.shape[0]
    columns_dev = parent_solution.shape[1]
    panel_width = inverse_one.shape[0]
    pivots = 2 * panel_width
    classes = pivots // TILE
    units = front_rhs.shape[0] // 8
    vmem = pl.BlockSpec(memory_space=pltpu.VMEM)
    smem = pl.BlockSpec(memory_space=pltpu.SMEM)
    hbm = pl.BlockSpec(memory_space=pltpu.HBM)
    dma = pltpu.SemaphoreType.DMA
    f32, bf16 = jnp.float32, jnp.bfloat16
    return pl.pallas_call(
        functools.partial(kernel, plane),
        out_shape=jax.ShapeDtypeStruct((front_rhs.shape[0], columns_dev), f32),
        in_specs=[smem, vmem, hbm, hbm, vmem, hbm, hbm, hbm],
        out_specs=vmem,
        scratch_shapes=[
            pltpu.VMEM((1, BLK), jnp.int32),
            pltpu.SMEM((1, BLK), jnp.int32),
            pltpu.VMEM((count, BLK, TILE), bf16),
            pltpu.VMEM((count, BLK, TILE), bf16),
            pltpu.VMEM((count, 1, BLK), jnp.int32),
            pltpu.VMEM((classes, count, BLK, TILE), bf16),
            pltpu.VMEM((count, 1, BLK), jnp.int32),
            pltpu.SMEM((count, 1, BLK), jnp.int32),
            pltpu.VMEM((rows_dev, columns_dev), bf16),
            pltpu.VMEM((rows_dev + 8, columns_dev), f32),
            pltpu.VMEM((BLK, columns_dev), f32),
            pltpu.VMEM((count, columns_dev, BLK), bf16),
            pltpu.VMEM((pivots, columns_dev), f32),
            pltpu.VMEM((4, columns_dev, 2 * TILE), f32),
            pltpu.VMEM((3, panel_width, panel_width), f32),
            pltpu.VMEM((pivots, pivots), bf16),
            pltpu.VMEM((pivots, pivots), bf16),
            pltpu.VMEM((units - 1, plane[0], plane[1], 8, columns_dev), f32),
            pltpu.VMEM((plane[1], plane[0], 8, columns_dev), f32),
            pltpu.VMEM((plane[0], 8, columns_dev), f32),
            pltpu.VMEM((units - 1, plane[1], 8, columns_dev), f32),
            pltpu.VMEM((units - 1, plane[0] - 1, plane[1], 8, columns_dev), f32),
            pltpu.VMEM((plane[1] - 1, plane[0], 8, columns_dev), f32),
            pltpu.VMEM((units - 1, plane[1] - 1, 8, columns_dev), f32),
            pltpu.VMEM((plane[0] - 1, 8, columns_dev), f32),
            dma((5,)),
            dma((2,)),
            dma((count,)),
            dma((count,)),
            dma((count,)),
            dma((count,)),
            dma((2, groups)),
            dma((2, groups)),
            dma((groups,)),
            dma((groups,)),
            dma((4, groups // BATCH)),
            dma((4, groups // BATCH)),
            dma((units - 1, plane[0] - 1)),
            dma((units - 1, plane[0] - 1)),
            dma((plane[1] - 1,)),
            dma((plane[1] - 1,)),
            dma((units - 1, plane[1] - 1)),
            dma((units - 1, plane[1] - 1)),
            dma((plane[0] - 1,)),
            dma((plane[0] - 1,)),
        ],
        compiler_params=pltpu.CompilerParams(
            collective_id=0, has_side_effects=True, vmem_limit_bytes=VMEM_BYTES
        ),
    )(
        live_counts,
        parent_rows.reshape(count, BLK),
        lower_panels.reshape(count, BLK, TILE),
        parent_solution,
        front_rhs,
        coupling,
        inverse_one,
        inverse_two,
    )


def solution(mesh):
    return jax.shard_map(
        body,
        mesh=mesh,
        in_specs=(
            P("rows", "rhs"),
            P("rows", "rhs"),
            P("rows"),
            P("rows"),
            P("rows", "rhs"),
            P(),
            P(),
            P(),
        ),
        out_specs=P("rows", "rhs"),
        check_vma=False,
    )
```

```python
import functools

import jax
import jax.numpy as jnp
from jax import lax
from jax.experimental import pallas as pl
from jax.experimental.pallas import tpu as pltpu
from jax.sharding import PartitionSpec as P

BLK = 128
TILE = 128
PLANE = (4, 8)
RING = 4
GROUP = 4
BATCH = 2
AHEAD = 2
VMEM_BYTES = 66781184
MESH = pl.DeviceIdType.MESH


def offsets(plane):
    size_y, size_z = plane
    pairs = [(dy, dz) for dy in range(size_y) for dz in range(size_z)]
    return sorted(
        pairs, key=lambda p: (min(p[1], size_z - p[1]), min(p[0], size_y - p[0]), p)
    )


def split(value):
    high = value.astype(jnp.bfloat16)
    low = (value - high.astype(jnp.float32)).astype(jnp.bfloat16)
    return high, low


def dot_split(left, right):
    def dot(a, b):
        return jnp.dot(a, b, preferred_element_type=jnp.float32)

    return dot(left[0], right[0]) + (dot(left[0], right[1]) + dot(left[1], right[0]))


def kernel(
    plane,
    live_ref,
    lists_ref,
    lower_hbm,
    parent_ref,
    rhs_ref,
    coupling_hbm,
    inverse_one_hbm,
    inverse_two_hbm,
    out_ref,
    order_buf,
    order_ref,
    held,
    blocks_ref,
    rows_ref,
    panels,
    row_buf,
    row_smem,
    staged,
    wide,
    picked,
    fetched,
    product,
    answer,
    partial,
    matrices,
    high,
    low,
    first_y,
    first_z,
    second_y,
    second_z,
    got_y,
    got_z,
    got_yz,
    got_zy,
    load_sem,
    smem_sem,
    row_send,
    row_recv,
    blk_send,
    blk_recv,
    near_send,
    near_recv,
    far_send,
    far_recv,
    twin_send,
    twin_recv,
    y_send,
    y_recv,
    z_send,
    z_recv,
    yz_send,
    yz_recv,
    zy_send,
    zy_recv,
):
    size_y, size_z = plane
    count = size_y * size_z
    groups = count // GROUP
    offs = offsets(plane)
    me = lax.axis_index("rows")
    side = lax.axis_index("rhs")
    y, z = me // size_z, me % size_z
    x, core = side // 2, side % 2
    right = ((x + 1) % RING) * 2 + core
    left = ((x + RING - 1) % RING) * 2 + core
    opposite = ((x + 2) % RING) * 2 + core
    twin = x * 2 + (1 - core)

    def target(t):
        dy, dz = offs[t]
        return ((y + size_y - dy) % size_y) * size_z + (z + size_z - dz) % size_z

    def source(t):
        dy, dz = offs[t]
        return ((y + dy) % size_y) * size_z + (z + dz) % size_z

    def remote(src, dst, send, recv, **device):
        return pltpu.make_async_remote_copy(
            src_ref=src, dst_ref=dst, send_sem=send, recv_sem=recv,
            device_id=device, device_id_type=MESH,
        )

    barrier = pltpu.get_barrier_semaphore()
    for t in range(1, count):
        pl.semaphore_signal(barrier, inc=1, device_id={"rows": target(t)}, device_id_type=MESH)
    for other in (left, right, twin):
        pl.semaphore_signal(barrier, inc=1, device_id={"rhs": other}, device_id_type=MESH)

    loads = [
        pltpu.make_async_copy(parent_ref, staged, load_sem.at[0]),
        pltpu.make_async_copy(coupling_hbm, matrices.at[0], load_sem.at[1]),
        pltpu.make_async_copy(inverse_one_hbm, matrices.at[1], load_sem.at[2]),
        pltpu.make_async_copy(inverse_two_hbm, matrices.at[2], load_sem.at[3]),
        pltpu.make_async_copy(lower_hbm, held, load_sem.at[4]),
    ]
    loads[4].start()
    for load in loads[:4]:
        load.start()
    rows_dev = staged.shape[0]
    lane = lax.broadcasted_iota(jnp.int32, (1, BLK), 1)
    owner = lax.div(lists_ref[:, 0:1], jnp.int32(rows_dev))
    number = lax.broadcasted_iota(jnp.int32, (count, BLK), 0)
    order_buf[...] = jnp.max(jnp.where(owner == lane, number, 0), axis=0, keepdims=True)
    to_order = pltpu.make_async_copy(order_buf, order_ref, smem_sem.at[1])
    to_order.start()
    to_order.wait()
    loads[4].wait()

    def arrange(index, carry):
        block = order_ref[0, index]
        blocks_ref[index] = held[block]
        alive = lane + block * BLK < live_ref[0]
        local = lax.rem(lists_ref[pl.ds(block, 1), :], jnp.int32(rows_dev))
        rows_ref[index] = jnp.where(alive, local, rows_dev)
        return carry

    lax.fori_loop(0, count, arrange, 0)
    panels[side, 0] = blocks_ref[me]
    row_buf[0] = rows_ref[me]

    pl.semaphore_wait(barrier, count + 2)

    row_copies, blk_copies = [], []
    for t in range(1, count):
        copy = remote(rows_ref.at[target(t)], row_buf.at[t], row_send.at[t], row_recv.at[t], rows=target(t))
        copy.start()
        row_copies.append(copy)
    for t in range(1, count):
        copy = remote(
            blocks_ref.at[target(t)], panels.at[side, t], blk_send.at[t], blk_recv.at[t], rows=target(t)
        )
        copy.start()
        blk_copies.append(copy)

    loads[0].wait()
    depth = staged.shape[0]
    step = 256

    def widen(i, carry):
        at = pl.ds(pl.multiple_of(i * step, step), step)
        wide[at, :] = staged[at, :].astype(jnp.float32)
        return carry

    lax.fori_loop(0, depth // step, widen, 0)
    wide[depth:, :] = jnp.zeros((wide.shape[0] - depth, wide.shape[1]), jnp.float32)

    def part(cls, g):
        return panels.at[cls, pl.ds(g * GROUP, GROUP)]

    def near(direction, cls, g):
        other = right if direction == 0 else left
        return remote(part(cls, g), part(cls, g), near_send.at[direction, g], near_recv.at[direction, g], rhs=other)

    def far(cls, g):
        other = right if g % 2 == 0 else left
        return remote(part(cls, g), part(cls, g), far_send.at[g], far_recv.at[g], rhs=other)

    def batch(cls, b):
        return panels.at[cls, pl.ds(b * BATCH * GROUP, BATCH * GROUP)]

    def pair(slot, cls, b):
        return remote(batch(cls, b), batch(cls, b), twin_send.at[slot, b], twin_recv.at[slot, b], rhs=twin)

    def share_twin(slot, cls, g):
        if (g + 1) % BATCH == 0:
            pair(slot, cls, g // BATCH).start()

    def take_rows():
        for copy in row_copies:
            copy.wait_recv()
        to_smem = pltpu.make_async_copy(row_buf, row_smem, smem_sem.at[0])
        to_smem.start()
        to_smem.wait()

    def gather(t):
        def eight(i, carry):
            for u in range(8):
                at = row_smem[t, 0, i * 8 + u]
                picked[pl.ds(i * 8 + u, 1), :] = wide[pl.ds(at, 1), :]
            return carry

        lax.fori_loop(0, BLK // 8, eight, 0)
        fetched[t] = picked[...].T.astype(jnp.bfloat16)

    def gather_group(g):
        def one(k, carry):
            gather(g * GROUP + k)
            return carry

        lax.fori_loop(0, GROUP, one, 0)

    acc_cols = fetched.shape[1]
    width = 2 * TILE
    chips = [x, (x + RING - 1) % RING, (x + 1) % RING, (x + 2) % RING]
    half = matrices.shape[1]

    def forward(g):
        for t in range(g * GROUP, (g + 1) * GROUP):
            if t > 0:
                blk_copies[t - 1].wait_recv()
        near(0, side, g).start()
        near(1, side, g).start()
        share_twin(0, side, g)

    def from_side(g):
        near(0, left, g).wait_recv()
        share_twin(1, left, g)
        near(1, right, g).wait_recv()
        share_twin(2, right, g)

    def relay(g):
        far(left if g % 2 == 0 else right, g).start()

    def from_far(g):
        far(opposite, g).wait_recv()
        share_twin(3, opposite, g)

    def term(slot, b):
        chip = chips[slot]
        pair(slot, chip * 2 + (1 - core), b).wait_recv()
        size = BATCH * GROUP
        at = pl.ds(b * size, size)
        lhs = jnp.concatenate([fetched[b * size + k] for k in range(size)], axis=1)
        rhs = jnp.concatenate(
            [panels[chip * 2 + c, at].reshape(size * BLK, TILE) for c in range(2)], axis=1
        )
        value = jnp.dot(lhs, rhs, preferred_element_type=jnp.float32)
        partial[slot] = value if b == 0 else partial[slot] + value

    def put(rows, columns, value):
        top, bottom = split(value)
        high[rows, columns] = top
        low[rows, columns] = bottom

    upper, lower = slice(0, half), slice(half, 2 * half)

    def invert(stage):
        if stage == 0:
            for load in loads[1:4]:
                load.wait()
            put(upper, upper, matrices[1])
            put(lower, lower, matrices[2])
            put(lower, upper, matrices[0])
        if stage == 1:
            put(upper, lower, dot_split(
                (high[lower, upper], low[lower, upper]), (high[lower, lower], low[lower, lower])
            ))
        if stage == 2:
            put(upper, lower, -dot_split(
                (high[upper, upper], low[upper, upper]), (high[upper, lower], low[upper, lower])
            ))
            high[lower, upper] = jnp.zeros((half, half), jnp.bfloat16)
            low[lower, upper] = jnp.zeros((half, half), jnp.bfloat16)

    share = rhs_ref.shape[0]

    def pivots(slot):
        return pl.ds(pl.multiple_of(chips[slot] * width, width), width)

    def solved(slot):
        value = product[pivots(slot), :] - partial[slot].T
        return dot_split((high[:, pivots(slot)], low[:, pivots(slot)]), split(value))

    ahead = min(AHEAD, groups - 3)
    for g in range(groups + 4):
        if g == groups - 1:
            for k in range(ahead):
                relay(k)
        if g < groups:
            forward(g)
        if g == 1:
            take_rows()
        if 2 <= g < groups + 2:
            from_side(g - 2)
        if g == groups:
            for k in range(ahead, groups - 1):
                relay(k)
        if g == groups + 1:
            relay(groups - 1)
        if 1 <= g <= groups:
            gather_group(g - 1)
        if g == groups - 4:
            invert(0)
            product[...] = jnp.zeros_like(product)
            own = pl.ds(pl.multiple_of(me * share, share), share)
            product[own, :] = rhs_ref[...].astype(jnp.float32)
        if g == groups - 3:
            invert(1)
        if g == groups - 2:
            invert(2)
        if 3 <= g < groups + 3 and (g - 2) % BATCH == 0:
            term(0, (g - 3) // BATCH)
        if g >= 4 and (g - 3) % BATCH == 0:
            term(1, (g - 4) // BATCH)
            term(2, (g - 4) // BATCH)

    batches = groups // BATCH
    from_far(0)
    answer[...] = solved(0)
    from_far(1)
    answer[...] = answer[...] + solved(1)
    from_far(2)
    from_far(3)
    answer[...] = answer[...] + solved(2)
    for g in range(4, groups):
        from_far(g)
        if g % BATCH == 0:
            term(3, g // BATCH - 2)
    term(3, batches - 2)
    term(3, batches - 1)

    units = share // 8
    stripes = units - 1
    total = answer[...] + solved(3)
    for r in range(count):
        index_y, index_z = divmod(r, size_z)
        for u in range(units):
            rows = total[r * share + u * 8 : r * share + u * 8 + 8]
            if u < stripes:
                first_y[u, index_y, index_z] = rows
            else:
                first_z[index_z, index_y] = rows

    y_copies, z_copies, yz_copies, zy_copies = [], [], [], []
    for u in range(stripes):
        for dy in range(1, size_y):
            to = (y + size_y - dy) % size_y
            copy = remote(
                first_y.at[u, to], got_y.at[u, dy - 1], y_send.at[u, dy - 1], y_recv.at[u, dy - 1],
                rows=to * size_z + z,
            )
            copy.start()
            y_copies.append(copy)
        if u == 0:
            for dz in range(1, size_z):
                to = (z + size_z - dz) % size_z
                copy = remote(
                    first_z.at[to], got_z.at[dz - 1], z_send.at[dz - 1], z_recv.at[dz - 1],
                    rows=y * size_z + to,
                )
                copy.start()
                z_copies.append(copy)

    def reduce_y(u):
        total = first_y[u, y]
        for dy in range(1, size_y):
            y_copies[u * (size_y - 1) + dy - 1].wait_recv()
            total = total + got_y[u, dy - 1]
        second_z[u] = total
        for dz in range(1, size_z):
            to = (z + size_z - dz) % size_z
            copy = remote(
                second_z.at[u, to], got_yz.at[u, dz - 1], yz_send.at[u, dz - 1], yz_recv.at[u, dz - 1],
                rows=y * size_z + to,
            )
            copy.start()
            yz_copies.append(copy)

    def reduce_z():
        total = first_z[z]
        for dz in range(1, size_z):
            z_copies[dz - 1].wait_recv()
            total = total + got_z[dz - 1]
        second_y[...] = total
        for dy in range(1, size_y):
            to = (y + size_y - dy) % size_y
            copy = remote(
                second_y.at[to], got_zy.at[dy - 1], zy_send.at[dy - 1], zy_recv.at[dy - 1],
                rows=to * size_z + z,
            )
            copy.start()
            zy_copies.append(copy)

    for u in range(stripes - 1):
        reduce_y(u)
    reduce_z()
    reduce_y(stripes - 1)
    for u in range(stripes):
        total = second_z[u, z]
        for dz in range(1, size_z):
            yz_copies[u * (size_z - 1) + dz - 1].wait_recv()
            total = total + got_yz[u, dz - 1]
        out_ref[u * 8 : u * 8 + 8, :] = total
    total = second_y[y]
    for copy, dy in zip(zy_copies, range(1, size_y)):
        copy.wait_recv()
        total = total + got_zy[dy - 1]
    out_ref[stripes * 8 :, :] = total

    for copy in row_copies + blk_copies + y_copies + z_copies + yz_copies + zy_copies:
        copy.wait_send()
    for g in range(groups):
        near(0, side, g).wait_send()
        near(1, side, g).wait_send()
        far(left if g % 2 == 0 else right, g).wait_send()
    for slot, cls in enumerate((side, left, right, opposite)):
        for b in range(batches):
            pair(slot, cls, b).wait_send()


def body(
    lower_panels,
    parent_solution,
    parent_rows,
    live_counts,
    front_rhs,
    coupling,
    inverse_one,
    inverse_two,
    plane=PLANE,
):
    count = plane[0] * plane[1]
    groups = count // GROUP
    rows_dev = parent_rows.shape[0]
    columns_dev = parent_solution.shape[1]
    panel_width = inverse_one.shape[0]
    pivots = 2 * panel_width
    classes = pivots // TILE
    units = front_rhs.shape[0] // 8
    vmem = pl.BlockSpec(memory_space=pltpu.VMEM)
    smem = pl.BlockSpec(memory_space=pltpu.SMEM)
    hbm = pl.BlockSpec(memory_space=pltpu.HBM)
    dma = pltpu.SemaphoreType.DMA
    f32, bf16 = jnp.float32, jnp.bfloat16
    return pl.pallas_call(
        functools.partial(kernel, plane),
        out_shape=jax.ShapeDtypeStruct((front_rhs.shape[0], columns_dev), f32),
        in_specs=[smem, vmem, hbm, hbm, vmem, hbm, hbm, hbm],
        out_specs=vmem,
        scratch_shapes=[
            pltpu.VMEM((1, BLK), jnp.int32),
            pltpu.SMEM((1, BLK), jnp.int32),
            pltpu.VMEM((count, BLK, TILE), bf16),
            pltpu.VMEM((count, BLK, TILE), bf16),
            pltpu.VMEM((count, 1, BLK), jnp.int32),
            pltpu.VMEM((classes, count, BLK, TILE), bf16),
            pltpu.VMEM((count, 1, BLK), jnp.int32),
            pltpu.SMEM((count, 1, BLK), jnp.int32),
            pltpu.VMEM((rows_dev, columns_dev), bf16),
            pltpu.VMEM((rows_dev + 8, columns_dev), f32),
            pltpu.VMEM((BLK, columns_dev), f32),
            pltpu.VMEM((count, columns_dev, BLK), bf16),
            pltpu.VMEM((pivots, columns_dev), f32),
            pltpu.VMEM((pivots, columns_dev), f32),
            pltpu.VMEM((4, columns_dev, 2 * TILE), f32),
            pltpu.VMEM((3, panel_width, panel_width), f32),
            pltpu.VMEM((pivots, pivots), bf16),
            pltpu.VMEM((pivots, pivots), bf16),
            pltpu.VMEM((units - 1, plane[0], plane[1], 8, columns_dev), f32),
            pltpu.VMEM((plane[1], plane[0], 8, columns_dev), f32),
            pltpu.VMEM((plane[0], 8, columns_dev), f32),
            pltpu.VMEM((units - 1, plane[1], 8, columns_dev), f32),
            pltpu.VMEM((units - 1, plane[0] - 1, plane[1], 8, columns_dev), f32),
            pltpu.VMEM((plane[1] - 1, plane[0], 8, columns_dev), f32),
            pltpu.VMEM((units - 1, plane[1] - 1, 8, columns_dev), f32),
            pltpu.VMEM((plane[0] - 1, 8, columns_dev), f32),
            dma((5,)),
            dma((2,)),
            dma((count,)),
            dma((count,)),
            dma((count,)),
            dma((count,)),
            dma((2, groups)),
            dma((2, groups)),
            dma((groups,)),
            dma((groups,)),
            dma((4, groups // BATCH)),
            dma((4, groups // BATCH)),
            dma((units - 1, plane[0] - 1)),
            dma((units - 1, plane[0] - 1)),
            dma((plane[1] - 1,)),
            dma((plane[1] - 1,)),
            dma((units - 1, plane[1] - 1)),
            dma((units - 1, plane[1] - 1)),
            dma((plane[0] - 1,)),
            dma((plane[0] - 1,)),
        ],
        compiler_params=pltpu.CompilerParams(
            collective_id=0, has_side_effects=True, vmem_limit_bytes=VMEM_BYTES
        ),
    )(
        live_counts,
        parent_rows.reshape(count, BLK),
        lower_panels.reshape(count, BLK, TILE),
        parent_solution,
        front_rhs,
        coupling,
        inverse_one,
        inverse_two,
    )


def solution(mesh):
    return jax.shard_map(
        body,
        mesh=mesh,
        in_specs=(
            P("rows", "rhs"),
            P("rows", "rhs"),
            P("rows"),
            P("rows"),
            P("rows", "rhs"),
            P(),
            P(),
            P(),
        ),
        out_specs=P("rows", "rhs"),
        check_vma=False,
    )
```

```python
import functools

import jax
import jax.numpy as jnp
from jax import lax
from jax.experimental import pallas as pl
from jax.experimental.pallas import tpu as pltpu
from jax.sharding import PartitionSpec as P

BLK = 128
TILE = 128
PLANE = (4, 8)
RING = 4
GROUP = 4
BATCH = 2
AHEAD = 2
VMEM_BYTES = 56000000
MESH = pl.DeviceIdType.MESH


def offsets(plane):
    size_y, size_z = plane
    pairs = [(dy, dz) for dy in range(size_y) for dz in range(size_z)]
    return sorted(
        pairs, key=lambda p: (min(p[1], size_z - p[1]), min(p[0], size_y - p[0]), p)
    )


def split(value):
    high = value.astype(jnp.bfloat16)
    low = (value - high.astype(jnp.float32)).astype(jnp.bfloat16)
    return high, low


def dot_split(left, right):
    def dot(a, b):
        return jnp.dot(a, b, preferred_element_type=jnp.float32)

    return dot(left[0], right[0]) + (dot(left[0], right[1]) + dot(left[1], right[0]))


def kernel(
    plane,
    live_ref,
    lists_ref,
    lower_hbm,
    parent_ref,
    rhs_ref,
    coupling_hbm,
    inverse_one_hbm,
    inverse_two_hbm,
    out_ref,
    order_buf,
    order_ref,
    held,
    blocks_ref,
    rows_ref,
    panels,
    row_buf,
    row_smem,
    staged,
    wide,
    picked,
    fetched,
    product,
    answer,
    partial,
    matrices,
    high,
    low,
    first_y,
    first_z,
    second_y,
    second_z,
    got_y,
    got_z,
    got_yz,
    got_zy,
    load_sem,
    smem_sem,
    row_send,
    row_recv,
    blk_send,
    blk_recv,
    near_send,
    near_recv,
    far_send,
    far_recv,
    twin_send,
    twin_recv,
    y_send,
    y_recv,
    z_send,
    z_recv,
    yz_send,
    yz_recv,
    zy_send,
    zy_recv,
):
    size_y, size_z = plane
    count = size_y * size_z
    groups = count // GROUP
    offs = offsets(plane)
    me = lax.axis_index("rows")
    side = lax.axis_index("rhs")
    y, z = me // size_z, me % size_z
    x, core = side // 2, side % 2
    right = ((x + 1) % RING) * 2 + core
    left = ((x + RING - 1) % RING) * 2 + core
    opposite = ((x + 2) % RING) * 2 + core
    twin = x * 2 + (1 - core)

    def target(t):
        dy, dz = offs[t]
        return ((y + size_y - dy) % size_y) * size_z + (z + size_z - dz) % size_z

    def source(t):
        dy, dz = offs[t]
        return ((y + dy) % size_y) * size_z + (z + dz) % size_z

    def remote(src, dst, send, recv, **device):
        return pltpu.make_async_remote_copy(
            src_ref=src, dst_ref=dst, send_sem=send, recv_sem=recv,
            device_id=device, device_id_type=MESH,
        )

    barrier = pltpu.get_barrier_semaphore()
    for t in range(1, count):
        pl.semaphore_signal(barrier, inc=1, device_id={"rows": target(t)}, device_id_type=MESH)
    for other in (left, right, twin):
        pl.semaphore_signal(barrier, inc=1, device_id={"rhs": other}, device_id_type=MESH)

    loads = [
        pltpu.make_async_copy(parent_ref, staged, load_sem.at[0]),
        pltpu.make_async_copy(coupling_hbm, matrices.at[0], load_sem.at[1]),
        pltpu.make_async_copy(inverse_one_hbm, matrices.at[1], load_sem.at[2]),
        pltpu.make_async_copy(inverse_two_hbm, matrices.at[2], load_sem.at[3]),
        pltpu.make_async_copy(lower_hbm, held, load_sem.at[4]),
    ]
    loads[4].start()
    for load in loads[:4]:
        load.start()
    rows_dev = staged.shape[0]
    lane = lax.broadcasted_iota(jnp.int32, (1, BLK), 1)
    owner = lax.div(lists_ref[:, 0:1], jnp.int32(rows_dev))
    number = lax.broadcasted_iota(jnp.int32, (count, BLK), 0)
    order_buf[...] = jnp.max(jnp.where(owner == lane, number, 0), axis=0, keepdims=True)
    to_order = pltpu.make_async_copy(order_buf, order_ref, smem_sem.at[1])
    to_order.start()
    to_order.wait()
    loads[4].wait()

    def arrange(index, carry):
        block = order_ref[0, index]
        blocks_ref[index] = held[block]
        alive = lane + block * BLK < live_ref[0]
        local = lax.rem(lists_ref[pl.ds(block, 1), :], jnp.int32(rows_dev))
        rows_ref[index] = jnp.where(alive, local, rows_dev)
        return carry

    lax.fori_loop(0, count, arrange, 0)
    panels[side, 0] = blocks_ref[me]
    row_buf[0] = rows_ref[me]

    pl.semaphore_wait(barrier, count + 2)

    row_copies, blk_copies = [], []
    for t in range(1, count):
        copy = remote(rows_ref.at[target(t)], row_buf.at[t], row_send.at[t], row_recv.at[t], rows=target(t))
        copy.start()
        row_copies.append(copy)
    for t in range(1, count):
        copy = remote(
            blocks_ref.at[target(t)], panels.at[side, t], blk_send.at[t], blk_recv.at[t], rows=target(t)
        )
        copy.start()
        blk_copies.append(copy)

    loads[0].wait()
    depth = staged.shape[0]
    step = 256

    def widen(i, carry):
        at = pl.ds(pl.multiple_of(i * step, step), step)
        wide[at, :] = staged[at, :].astype(jnp.float32)
        return carry

    lax.fori_loop(0, depth // step, widen, 0)
    wide[depth:, :] = jnp.zeros((wide.shape[0] - depth, wide.shape[1]), jnp.float32)

    def part(cls, g):
        return panels.at[cls, pl.ds(g * GROUP, GROUP)]

    def near(direction, cls, g):
        other = right if direction == 0 else left
        return remote(part(cls, g), part(cls, g), near_send.at[direction, g], near_recv.at[direction, g], rhs=other)

    def far(cls, g):
        other = right if g % 2 == 0 else left
        return remote(part(cls, g), part(cls, g), far_send.at[g], far_recv.at[g], rhs=other)

    def batch(cls, b):
        return panels.at[cls, pl.ds(b * BATCH * GROUP, BATCH * GROUP)]

    def pair(slot, cls, b):
        return remote(batch(cls, b), batch(cls, b), twin_send.at[slot, b], twin_recv.at[slot, b], rhs=twin)

    def share_twin(slot, cls, g):
        if (g + 1) % BATCH == 0:
            pair(slot, cls, g // BATCH).start()

    def take_rows():
        for copy in row_copies:
            copy.wait_recv()
        to_smem = pltpu.make_async_copy(row_buf, row_smem, smem_sem.at[0])
        to_smem.start()
        to_smem.wait()

    def gather(t):
        def eight(i, carry):
            for u in range(8):
                at = row_smem[t, 0, i * 8 + u]
                picked[pl.ds(i * 8 + u, 1), :] = wide[pl.ds(at, 1), :]
            return carry

        lax.fori_loop(0, BLK // 8, eight, 0)
        fetched[t] = picked[...].T.astype(jnp.bfloat16)

    def gather_group(g):
        def one(k, carry):
            gather(g * GROUP + k)
            return carry

        lax.fori_loop(0, GROUP, one, 0)

    acc_cols = fetched.shape[1]
    width = 2 * TILE
    chips = [x, (x + RING - 1) % RING, (x + 1) % RING, (x + 2) % RING]
    half = matrices.shape[1]

    def forward(g):
        for t in range(g * GROUP, (g + 1) * GROUP):
            if t > 0:
                blk_copies[t - 1].wait_recv()
        near(0, side, g).start()
        near(1, side, g).start()
        share_twin(0, side, g)

    def from_side(g):
        near(0, left, g).wait_recv()
        share_twin(1, left, g)
        near(1, right, g).wait_recv()
        share_twin(2, right, g)

    def relay(g):
        far(left if g % 2 == 0 else right, g).start()

    def from_far(g):
        far(opposite, g).wait_recv()
        share_twin(3, opposite, g)

    def term(slot, b):
        chip = chips[slot]
        pair(slot, chip * 2 + (1 - core), b).wait_recv()
        size = BATCH * GROUP
        at = pl.ds(b * size, size)
        lhs = jnp.concatenate([fetched[b * size + k] for k in range(size)], axis=1)
        rhs = jnp.concatenate(
            [panels[chip * 2 + c, at].reshape(size * BLK, TILE) for c in range(2)], axis=1
        )
        value = jnp.dot(lhs, rhs, preferred_element_type=jnp.float32)
        partial[slot] = value if b == 0 else partial[slot] + value

    def put(rows, columns, value):
        top, bottom = split(value)
        high[rows, columns] = top
        low[rows, columns] = bottom

    upper, lower = slice(0, half), slice(half, 2 * half)

    def invert(stage):
        if stage == 0:
            for load in loads[1:4]:
                load.wait()
            put(upper, upper, matrices[1])
            put(lower, lower, matrices[2])
            put(lower, upper, matrices[0])
        if stage == 1:
            put(upper, lower, dot_split(
                (high[lower, upper], low[lower, upper]), (high[lower, lower], low[lower, lower])
            ))
        if stage == 2:
            put(upper, lower, -dot_split(
                (high[upper, upper], low[upper, upper]), (high[upper, lower], low[upper, lower])
            ))
            high[lower, upper] = jnp.zeros((half, half), jnp.bfloat16)
            low[lower, upper] = jnp.zeros((half, half), jnp.bfloat16)

    share = rhs_ref.shape[0]

    def pivots(slot):
        return pl.ds(pl.multiple_of(chips[slot] * width, width), width)

    def solved(slot):
        value = product[pivots(slot), :] - partial[slot].T
        return dot_split((high[:, pivots(slot)], low[:, pivots(slot)]), split(value))

    ahead = min(AHEAD, groups - 3)
    for g in range(groups + 4):
        if g == groups - 1:
            for k in range(ahead):
                relay(k)
        if g < groups:
            forward(g)
        if g == 1:
            take_rows()
        if 2 <= g < groups + 2:
            from_side(g - 2)
        if g == groups:
            for k in range(ahead, groups - 1):
                relay(k)
        if g == groups + 1:
            relay(groups - 1)
        if 1 <= g <= groups:
            gather_group(g - 1)
        if g == groups - 4:
            invert(0)
            product[...] = jnp.zeros_like(product)
            own = pl.ds(pl.multiple_of(me * share, share), share)
            product[own, :] = rhs_ref[...].astype(jnp.float32)
        if g == groups - 3:
            invert(1)
        if g == groups - 2:
            invert(2)
        if 3 <= g < groups + 3 and (g - 2) % BATCH == 0:
            term(0, (g - 3) // BATCH)
        if g >= 4 and (g - 3) % BATCH == 0:
            term(1, (g - 4) // BATCH)
            term(2, (g - 4) // BATCH)

    batches = groups // BATCH
    from_far(0)
    answer[...] = solved(0)
    from_far(1)
    answer[...] = answer[...] + solved(1)
    from_far(2)
    from_far(3)
    answer[...] = answer[...] + solved(2)
    for g in range(4, groups):
        from_far(g)
        if g % BATCH == 0:
            term(3, g // BATCH - 2)
    term(3, batches - 2)
    term(3, batches - 1)

    units = share // 8
    stripes = units - 1
    total = answer[...] + solved(3)
    for r in range(count):
        index_y, index_z = divmod(r, size_z)
        for u in range(units):
            rows = total[r * share + u * 8 : r * share + u * 8 + 8]
            if u < stripes:
                first_y[u, index_y, index_z] = rows
            else:
                first_z[index_z, index_y] = rows

    y_copies, z_copies, yz_copies, zy_copies = [], [], [], []
    for u in range(stripes):
        for dy in range(1, size_y):
            to = (y + size_y - dy) % size_y
            copy = remote(
                first_y.at[u, to], got_y.at[u, dy - 1], y_send.at[u, dy - 1], y_recv.at[u, dy - 1],
                rows=to * size_z + z,
            )
            copy.start()
            y_copies.append(copy)
        if u == 0:
            for dz in range(1, size_z):
                to = (z + size_z - dz) % size_z
                copy = remote(
                    first_z.at[to], got_z.at[dz - 1], z_send.at[dz - 1], z_recv.at[dz - 1],
                    rows=y * size_z + to,
                )
                copy.start()
                z_copies.append(copy)

    def reduce_y(u):
        total = first_y[u, y]
        for dy in range(1, size_y):
            y_copies[u * (size_y - 1) + dy - 1].wait_recv()
            total = total + got_y[u, dy - 1]
        second_z[u] = total
        for dz in range(1, size_z):
            to = (z + size_z - dz) % size_z
            copy = remote(
                second_z.at[u, to], got_yz.at[u, dz - 1], yz_send.at[u, dz - 1], yz_recv.at[u, dz - 1],
                rows=y * size_z + to,
            )
            copy.start()
            yz_copies.append(copy)

    def reduce_z():
        total = first_z[z]
        for dz in range(1, size_z):
            z_copies[dz - 1].wait_recv()
            total = total + got_z[dz - 1]
        second_y[...] = total
        for dy in range(1, size_y):
            to = (y + size_y - dy) % size_y
            copy = remote(
                second_y.at[to], got_zy.at[dy - 1], zy_send.at[dy - 1], zy_recv.at[dy - 1],
                rows=to * size_z + z,
            )
            copy.start()
            zy_copies.append(copy)

    for u in range(stripes - 1):
        reduce_y(u)
    reduce_z()
    reduce_y(stripes - 1)
    for u in range(stripes):
        total = second_z[u, z]
        for dz in range(1, size_z):
            yz_copies[u * (size_z - 1) + dz - 1].wait_recv()
            total = total + got_yz[u, dz - 1]
        out_ref[u * 8 : u * 8 + 8, :] = total
    total = second_y[y]
    for copy, dy in zip(zy_copies, range(1, size_y)):
        copy.wait_recv()
        total = total + got_zy[dy - 1]
    out_ref[stripes * 8 :, :] = total

    for copy in row_copies + blk_copies + y_copies + z_copies + yz_copies + zy_copies:
        copy.wait_send()
    for g in range(groups):
        near(0, side, g).wait_send()
        near(1, side, g).wait_send()
        far(left if g % 2 == 0 else right, g).wait_send()
    for slot, cls in enumerate((side, left, right, opposite)):
        for b in range(batches):
            pair(slot, cls, b).wait_send()


def body(
    lower_panels,
    parent_solution,
    parent_rows,
    live_counts,
    front_rhs,
    coupling,
    inverse_one,
    inverse_two,
    plane=PLANE,
):
    count = plane[0] * plane[1]
    groups = count // GROUP
    rows_dev = parent_rows.shape[0]
    columns_dev = parent_solution.shape[1]
    panel_width = inverse_one.shape[0]
    pivots = 2 * panel_width
    classes = pivots // TILE
    units = front_rhs.shape[0] // 8
    vmem = pl.BlockSpec(memory_space=pltpu.VMEM)
    smem = pl.BlockSpec(memory_space=pltpu.SMEM)
    hbm = pl.BlockSpec(memory_space=pltpu.HBM)
    dma = pltpu.SemaphoreType.DMA
    f32, bf16 = jnp.float32, jnp.bfloat16
    return pl.pallas_call(
        functools.partial(kernel, plane),
        out_shape=jax.ShapeDtypeStruct((front_rhs.shape[0], columns_dev), f32),
        in_specs=[smem, vmem, hbm, hbm, vmem, hbm, hbm, hbm],
        out_specs=vmem,
        scratch_shapes=[
            pltpu.VMEM((1, BLK), jnp.int32),
            pltpu.SMEM((1, BLK), jnp.int32),
            pltpu.VMEM((count, BLK, TILE), bf16),
            pltpu.VMEM((count, BLK, TILE), bf16),
            pltpu.VMEM((count, 1, BLK), jnp.int32),
            pltpu.VMEM((classes, count, BLK, TILE), bf16),
            pltpu.VMEM((count, 1, BLK), jnp.int32),
            pltpu.SMEM((count, 1, BLK), jnp.int32),
            pltpu.VMEM((rows_dev, columns_dev), bf16),
            pltpu.VMEM((rows_dev + 8, columns_dev), f32),
            pltpu.VMEM((BLK, columns_dev), f32),
            pltpu.VMEM((count, columns_dev, BLK), bf16),
            pltpu.VMEM((pivots, columns_dev), f32),
            pltpu.VMEM((pivots, columns_dev), f32),
            pltpu.VMEM((4, columns_dev, 2 * TILE), f32),
            pltpu.VMEM((3, panel_width, panel_width), f32),
            pltpu.VMEM((pivots, pivots), bf16),
            pltpu.VMEM((pivots, pivots), bf16),
            pltpu.VMEM((units - 1, plane[0], plane[1], 8, columns_dev), f32),
            pltpu.VMEM((plane[1], plane[0], 8, columns_dev), f32),
            pltpu.VMEM((plane[0], 8, columns_dev), f32),
            pltpu.VMEM((units - 1, plane[1], 8, columns_dev), f32),
            pltpu.VMEM((units - 1, plane[0] - 1, plane[1], 8, columns_dev), f32),
            pltpu.VMEM((plane[1] - 1, plane[0], 8, columns_dev), f32),
            pltpu.VMEM((units - 1, plane[1] - 1, 8, columns_dev), f32),
            pltpu.VMEM((plane[0] - 1, 8, columns_dev), f32),
            dma((5,)),
            dma((2,)),
            dma((count,)),
            dma((count,)),
            dma((count,)),
            dma((count,)),
            dma((2, groups)),
            dma((2, groups)),
            dma((groups,)),
            dma((groups,)),
            dma((4, groups // BATCH)),
            dma((4, groups // BATCH)),
            dma((units - 1, plane[0] - 1)),
            dma((units - 1, plane[0] - 1)),
            dma((plane[1] - 1,)),
            dma((plane[1] - 1,)),
            dma((units - 1, plane[1] - 1)),
            dma((units - 1, plane[1] - 1)),
            dma((plane[0] - 1,)),
            dma((plane[0] - 1,)),
        ],
        compiler_params=pltpu.CompilerParams(
            collective_id=0, has_side_effects=True, vmem_limit_bytes=VMEM_BYTES
        ),
    )(
        live_counts,
        parent_rows.reshape(count, BLK),
        lower_panels.reshape(count, BLK, TILE),
        parent_solution,
        front_rhs,
        coupling,
        inverse_one,
        inverse_two,
    )


def solution(mesh):
    return jax.shard_map(
        body,
        mesh=mesh,
        in_specs=(
            P("rows", "rhs"),
            P("rows", "rhs"),
            P("rows"),
            P("rows"),
            P("rows", "rhs"),
            P(),
            P(),
            P(),
        ),
        out_specs=P("rows", "rhs"),
        check_vma=False,
    )
```

```python
import functools

import jax
import jax.numpy as jnp
from jax import lax
from jax.experimental import pallas as pl
from jax.experimental.pallas import tpu as pltpu
from jax.sharding import PartitionSpec as P

BLK = 128
TILE = 128
PLANE = (4, 8)
RING = 4
GROUP = 4
BATCH = 2
AHEAD = 2
INVAT = 4
ZFIRST = 1
VMEM_BYTES = 56000000
MESH = pl.DeviceIdType.MESH


def offsets(plane):
    size_y, size_z = plane
    pairs = [(dy, dz) for dy in range(size_y) for dz in range(size_z)]
    return sorted(
        pairs, key=lambda p: (min(p[1], size_z - p[1]), min(p[0], size_y - p[0]), p)
    )


def split(value):
    high = value.astype(jnp.bfloat16)
    low = (value - high.astype(jnp.float32)).astype(jnp.bfloat16)
    return high, low


def dot_split(left, right):
    def dot(a, b):
        return jnp.dot(a, b, preferred_element_type=jnp.float32)

    return dot(left[0], right[0]) + (dot(left[0], right[1]) + dot(left[1], right[0]))


def kernel(
    plane,
    live_ref,
    lists_ref,
    lower_hbm,
    parent_ref,
    rhs_ref,
    coupling_hbm,
    inverse_one_hbm,
    inverse_two_hbm,
    out_ref,
    order_buf,
    order_ref,
    held,
    blocks_ref,
    rows_ref,
    panels,
    row_buf,
    row_smem,
    staged,
    wide,
    picked,
    fetched,
    product,
    answer,
    partial,
    matrices,
    high,
    low,
    first_y,
    first_z,
    second_y,
    second_z,
    got_y,
    got_z,
    got_yz,
    got_zy,
    load_sem,
    smem_sem,
    row_send,
    row_recv,
    blk_send,
    blk_recv,
    near_send,
    near_recv,
    far_send,
    far_recv,
    twin_send,
    twin_recv,
    y_send,
    y_recv,
    z_send,
    z_recv,
    yz_send,
    yz_recv,
    zy_send,
    zy_recv,
):
    size_y, size_z = plane
    count = size_y * size_z
    groups = count // GROUP
    offs = offsets(plane)
    me = lax.axis_index("rows")
    side = lax.axis_index("rhs")
    y, z = me // size_z, me % size_z
    x, core = side // 2, side % 2
    right = ((x + 1) % RING) * 2 + core
    left = ((x + RING - 1) % RING) * 2 + core
    opposite = ((x + 2) % RING) * 2 + core
    twin = x * 2 + (1 - core)

    def target(t):
        dy, dz = offs[t]
        return ((y + size_y - dy) % size_y) * size_z + (z + size_z - dz) % size_z

    def source(t):
        dy, dz = offs[t]
        return ((y + dy) % size_y) * size_z + (z + dz) % size_z

    def remote(src, dst, send, recv, **device):
        return pltpu.make_async_remote_copy(
            src_ref=src, dst_ref=dst, send_sem=send, recv_sem=recv,
            device_id=device, device_id_type=MESH,
        )

    barrier = pltpu.get_barrier_semaphore()
    for t in range(1, count):
        pl.semaphore_signal(barrier, inc=1, device_id={"rows": target(t)}, device_id_type=MESH)
    for other in (left, right, twin):
        pl.semaphore_signal(barrier, inc=1, device_id={"rhs": other}, device_id_type=MESH)

    loads = [
        pltpu.make_async_copy(parent_ref, staged, load_sem.at[0]),
        pltpu.make_async_copy(coupling_hbm, matrices.at[0], load_sem.at[1]),
        pltpu.make_async_copy(inverse_one_hbm, matrices.at[1], load_sem.at[2]),
        pltpu.make_async_copy(inverse_two_hbm, matrices.at[2], load_sem.at[3]),
        pltpu.make_async_copy(lower_hbm, held, load_sem.at[4]),
    ]
    loads[4].start()
    for load in loads[:4]:
        load.start()
    rows_dev = staged.shape[0]
    lane = lax.broadcasted_iota(jnp.int32, (1, BLK), 1)
    owner = lax.div(lists_ref[:, 0:1], jnp.int32(rows_dev))
    number = lax.broadcasted_iota(jnp.int32, (count, BLK), 0)
    order_buf[...] = jnp.max(jnp.where(owner == lane, number, 0), axis=0, keepdims=True)
    to_order = pltpu.make_async_copy(order_buf, order_ref, smem_sem.at[1])
    to_order.start()
    to_order.wait()
    loads[4].wait()

    def arrange(index, carry):
        block = order_ref[0, index]
        blocks_ref[index] = held[block]
        alive = lane + block * BLK < live_ref[0]
        local = lax.rem(lists_ref[pl.ds(block, 1), :], jnp.int32(rows_dev))
        rows_ref[index] = jnp.where(alive, local, rows_dev)
        return carry

    lax.fori_loop(0, count, arrange, 0)
    panels[side, 0] = blocks_ref[me]
    row_buf[0] = rows_ref[me]

    pl.semaphore_wait(barrier, count + 2)

    row_copies, blk_copies = [], []
    for t in range(1, count):
        copy = remote(rows_ref.at[target(t)], row_buf.at[t], row_send.at[t], row_recv.at[t], rows=target(t))
        copy.start()
        row_copies.append(copy)
    for t in range(1, count):
        copy = remote(
            blocks_ref.at[target(t)], panels.at[side, t], blk_send.at[t], blk_recv.at[t], rows=target(t)
        )
        copy.start()
        blk_copies.append(copy)

    loads[0].wait()
    depth = staged.shape[0]
    step = 256

    def widen(i, carry):
        at = pl.ds(pl.multiple_of(i * step, step), step)
        wide[at, :] = staged[at, :].astype(jnp.float32)
        return carry

    lax.fori_loop(0, depth // step, widen, 0)
    wide[depth:, :] = jnp.zeros((wide.shape[0] - depth, wide.shape[1]), jnp.float32)

    def part(cls, g):
        return panels.at[cls, pl.ds(g * GROUP, GROUP)]

    def near(direction, cls, g):
        other = right if direction == 0 else left
        return remote(part(cls, g), part(cls, g), near_send.at[direction, g], near_recv.at[direction, g], rhs=other)

    def far(cls, g):
        other = right if g % 2 == 0 else left
        return remote(part(cls, g), part(cls, g), far_send.at[g], far_recv.at[g], rhs=other)

    def batch(cls, b):
        return panels.at[cls, pl.ds(b * BATCH * GROUP, BATCH * GROUP)]

    def pair(slot, cls, b):
        return remote(batch(cls, b), batch(cls, b), twin_send.at[slot, b], twin_recv.at[slot, b], rhs=twin)

    def share_twin(slot, cls, g):
        if (g + 1) % BATCH == 0:
            pair(slot, cls, g // BATCH).start()

    def take_rows():
        for copy in row_copies:
            copy.wait_recv()
        to_smem = pltpu.make_async_copy(row_buf, row_smem, smem_sem.at[0])
        to_smem.start()
        to_smem.wait()

    def gather(t):
        def eight(i, carry):
            for u in range(8):
                at = row_smem[t, 0, i * 8 + u]
                picked[pl.ds(i * 8 + u, 1), :] = wide[pl.ds(at, 1), :]
            return carry

        lax.fori_loop(0, BLK // 8, eight, 0)
        fetched[t] = picked[...].T.astype(jnp.bfloat16)

    def gather_group(g):
        def one(k, carry):
            gather(g * GROUP + k)
            return carry

        lax.fori_loop(0, GROUP, one, 0)

    acc_cols = fetched.shape[1]
    width = 2 * TILE
    chips = [x, (x + RING - 1) % RING, (x + 1) % RING, (x + 2) % RING]
    half = matrices.shape[1]

    def forward(g):
        for t in range(g * GROUP, (g + 1) * GROUP):
            if t > 0:
                blk_copies[t - 1].wait_recv()
        near(0, side, g).start()
        near(1, side, g).start()
        share_twin(0, side, g)

    def from_side(g):
        near(0, left, g).wait_recv()
        share_twin(1, left, g)
        near(1, right, g).wait_recv()
        share_twin(2, right, g)

    def relay(g):
        far(left if g % 2 == 0 else right, g).start()

    def from_far(g):
        far(opposite, g).wait_recv()
        share_twin(3, opposite, g)

    def term(slot, b):
        chip = chips[slot]
        pair(slot, chip * 2 + (1 - core), b).wait_recv()
        size = BATCH * GROUP
        at = pl.ds(b * size, size)
        lhs = jnp.concatenate([fetched[b * size + k] for k in range(size)], axis=1)
        rhs = jnp.concatenate(
            [panels[chip * 2 + c, at].reshape(size * BLK, TILE) for c in range(2)], axis=1
        )
        value = jnp.dot(lhs, rhs, preferred_element_type=jnp.float32)
        partial[slot] = value if b == 0 else partial[slot] + value

    def put(rows, columns, value):
        top, bottom = split(value)
        high[rows, columns] = top
        low[rows, columns] = bottom

    upper, lower = slice(0, half), slice(half, 2 * half)

    def invert(stage):
        if stage == 0:
            for load in loads[1:4]:
                load.wait()
            put(upper, upper, matrices[1])
            put(lower, lower, matrices[2])
            put(lower, upper, matrices[0])
        if stage == 1:
            put(upper, lower, dot_split(
                (high[lower, upper], low[lower, upper]), (high[lower, lower], low[lower, lower])
            ))
        if stage == 2:
            put(upper, lower, -dot_split(
                (high[upper, upper], low[upper, upper]), (high[upper, lower], low[upper, lower])
            ))
            high[lower, upper] = jnp.zeros((half, half), jnp.bfloat16)
            low[lower, upper] = jnp.zeros((half, half), jnp.bfloat16)

    share = rhs_ref.shape[0]

    def pivots(slot):
        return pl.ds(pl.multiple_of(chips[slot] * width, width), width)

    def solved(slot):
        value = product[pivots(slot), :] - partial[slot].T
        return dot_split((high[:, pivots(slot)], low[:, pivots(slot)]), split(value))

    ahead = min(AHEAD, groups - 3)
    for g in range(groups + 4):
        if g == groups - 1:
            for k in range(ahead):
                relay(k)
        if g < groups:
            forward(g)
        if g == 1:
            take_rows()
        if 2 <= g < groups + 2:
            from_side(g - 2)
        if g == groups:
            for k in range(ahead, groups - 1):
                relay(k)
        if g == groups + 1:
            relay(groups - 1)
        if 1 <= g <= groups:
            gather_group(g - 1)
        if g == INVAT:
            invert(0)
            product[...] = jnp.zeros_like(product)
            own = pl.ds(pl.multiple_of(me * share, share), share)
            product[own, :] = rhs_ref[...].astype(jnp.float32)
        if g == INVAT + 1:
            invert(1)
        if g == INVAT + 2:
            invert(2)
        if 3 <= g < groups + 3 and (g - 2) % BATCH == 0:
            term(0, (g - 3) // BATCH)
        if g >= 4 and (g - 3) % BATCH == 0:
            term(1, (g - 4) // BATCH)
            term(2, (g - 4) // BATCH)

    batches = groups // BATCH
    from_far(0)
    answer[...] = solved(0)
    from_far(1)
    answer[...] = answer[...] + solved(1)
    from_far(2)
    from_far(3)
    answer[...] = answer[...] + solved(2)
    for g in range(4, groups):
        from_far(g)
        if g % BATCH == 0:
            term(3, g // BATCH - 2)
    term(3, batches - 2)
    term(3, batches - 1)

    units = share // 8
    stripes = units - 1
    total = answer[...] + solved(3)
    for r in range(count):
        index_y, index_z = divmod(r, size_z)
        for u in range(units):
            rows = total[r * share + u * 8 : r * share + u * 8 + 8]
            if u < stripes:
                first_y[u, index_y, index_z] = rows
            else:
                first_z[index_z, index_y] = rows

    y_copies, z_copies, yz_copies, zy_copies = [], [], [], []
    def start_z():
        for dz in range(1, size_z):
            to = (z + size_z - dz) % size_z
            copy = remote(
                first_z.at[to], got_z.at[dz - 1], z_send.at[dz - 1], z_recv.at[dz - 1],
                rows=y * size_z + to,
            )
            copy.start()
            z_copies.append(copy)

    if ZFIRST:
        start_z()
    for u in range(stripes):
        for dy in range(1, size_y):
            to = (y + size_y - dy) % size_y
            copy = remote(
                first_y.at[u, to], got_y.at[u, dy - 1], y_send.at[u, dy - 1], y_recv.at[u, dy - 1],
                rows=to * size_z + z,
            )
            copy.start()
            y_copies.append(copy)
        if u == 0 and not ZFIRST:
            start_z()

    def reduce_y(u):
        total = first_y[u, y]
        for dy in range(1, size_y):
            y_copies[u * (size_y - 1) + dy - 1].wait_recv()
            total = total + got_y[u, dy - 1]
        second_z[u] = total
        for dz in range(1, size_z):
            to = (z + size_z - dz) % size_z
            copy = remote(
                second_z.at[u, to], got_yz.at[u, dz - 1], yz_send.at[u, dz - 1], yz_recv.at[u, dz - 1],
                rows=y * size_z + to,
            )
            copy.start()
            yz_copies.append(copy)

    def reduce_z():
        total = first_z[z]
        for dz in range(1, size_z):
            z_copies[dz - 1].wait_recv()
            total = total + got_z[dz - 1]
        second_y[...] = total
        for dy in range(1, size_y):
            to = (y + size_y - dy) % size_y
            copy = remote(
                second_y.at[to], got_zy.at[dy - 1], zy_send.at[dy - 1], zy_recv.at[dy - 1],
                rows=to * size_z + z,
            )
            copy.start()
            zy_copies.append(copy)

    for u in range(stripes - 1):
        reduce_y(u)
    reduce_z()
    reduce_y(stripes - 1)
    for u in range(stripes):
        total = second_z[u, z]
        for dz in range(1, size_z):
            yz_copies[u * (size_z - 1) + dz - 1].wait_recv()
            total = total + got_yz[u, dz - 1]
        out_ref[u * 8 : u * 8 + 8, :] = total
    total = second_y[y]
    for copy, dy in zip(zy_copies, range(1, size_y)):
        copy.wait_recv()
        total = total + got_zy[dy - 1]
    out_ref[stripes * 8 :, :] = total

    for copy in row_copies + blk_copies + y_copies + z_copies + yz_copies + zy_copies:
        copy.wait_send()
    for g in range(groups):
        near(0, side, g).wait_send()
        near(1, side, g).wait_send()
        far(left if g % 2 == 0 else right, g).wait_send()
    for slot, cls in enumerate((side, left, right, opposite)):
        for b in range(batches):
            pair(slot, cls, b).wait_send()


def body(
    lower_panels,
    parent_solution,
    parent_rows,
    live_counts,
    front_rhs,
    coupling,
    inverse_one,
    inverse_two,
    plane=PLANE,
):
    count = plane[0] * plane[1]
    groups = count // GROUP
    rows_dev = parent_rows.shape[0]
    columns_dev = parent_solution.shape[1]
    panel_width = inverse_one.shape[0]
    pivots = 2 * panel_width
    classes = pivots // TILE
    units = front_rhs.shape[0] // 8
    vmem = pl.BlockSpec(memory_space=pltpu.VMEM)
    smem = pl.BlockSpec(memory_space=pltpu.SMEM)
    hbm = pl.BlockSpec(memory_space=pltpu.HBM)
    dma = pltpu.SemaphoreType.DMA
    f32, bf16 = jnp.float32, jnp.bfloat16
    return pl.pallas_call(
        functools.partial(kernel, plane),
        out_shape=jax.ShapeDtypeStruct((front_rhs.shape[0], columns_dev), f32),
        in_specs=[smem, vmem, hbm, hbm, vmem, hbm, hbm, hbm],
        out_specs=vmem,
        scratch_shapes=[
            pltpu.VMEM((1, BLK), jnp.int32),
            pltpu.SMEM((1, BLK), jnp.int32),
            pltpu.VMEM((count, BLK, TILE), bf16),
            pltpu.VMEM((count, BLK, TILE), bf16),
            pltpu.VMEM((count, 1, BLK), jnp.int32),
            pltpu.VMEM((classes, count, BLK, TILE), bf16),
            pltpu.VMEM((count, 1, BLK), jnp.int32),
            pltpu.SMEM((count, 1, BLK), jnp.int32),
            pltpu.VMEM((rows_dev, columns_dev), bf16),
            pltpu.VMEM((rows_dev + 8, columns_dev), f32),
            pltpu.VMEM((BLK, columns_dev), f32),
            pltpu.VMEM((count, columns_dev, BLK), bf16),
            pltpu.VMEM((pivots, columns_dev), f32),
            pltpu.VMEM((pivots, columns_dev), f32),
            pltpu.VMEM((4, columns_dev, 2 * TILE), f32),
            pltpu.VMEM((3, panel_width, panel_width), f32),
            pltpu.VMEM((pivots, pivots), bf16),
            pltpu.VMEM((pivots, pivots), bf16),
            pltpu.VMEM((units - 1, plane[0], plane[1], 8, columns_dev), f32),
            pltpu.VMEM((plane[1], plane[0], 8, columns_dev), f32),
            pltpu.VMEM((plane[0], 8, columns_dev), f32),
            pltpu.VMEM((units - 1, plane[1], 8, columns_dev), f32),
            pltpu.VMEM((units - 1, plane[0] - 1, plane[1], 8, columns_dev), f32),
            pltpu.VMEM((plane[1] - 1, plane[0], 8, columns_dev), f32),
            pltpu.VMEM((units - 1, plane[1] - 1, 8, columns_dev), f32),
            pltpu.VMEM((plane[0] - 1, 8, columns_dev), f32),
            dma((5,)),
            dma((2,)),
            dma((count,)),
            dma((count,)),
            dma((count,)),
            dma((count,)),
            dma((2, groups)),
            dma((2, groups)),
            dma((groups,)),
            dma((groups,)),
            dma((4, groups // BATCH)),
            dma((4, groups // BATCH)),
            dma((units - 1, plane[0] - 1)),
            dma((units - 1, plane[0] - 1)),
            dma((plane[1] - 1,)),
            dma((plane[1] - 1,)),
            dma((units - 1, plane[1] - 1)),
            dma((units - 1, plane[1] - 1)),
            dma((plane[0] - 1,)),
            dma((plane[0] - 1,)),
        ],
        compiler_params=pltpu.CompilerParams(
            collective_id=0, has_side_effects=True, vmem_limit_bytes=VMEM_BYTES
        ),
    )(
        live_counts,
        parent_rows.reshape(count, BLK),
        lower_panels.reshape(count, BLK, TILE),
        parent_solution,
        front_rhs,
        coupling,
        inverse_one,
        inverse_two,
    )


def solution(mesh):
    return jax.shard_map(
        body,
        mesh=mesh,
        in_specs=(
            P("rows", "rhs"),
            P("rows", "rhs"),
            P("rows"),
            P("rows"),
            P("rows", "rhs"),
            P(),
            P(),
            P(),
        ),
        out_specs=P("rows", "rhs"),
        check_vma=False,
    )
```
